32 devices in a mesh: fsdp: 4 (over z), replica: 2 (over x), ctx: 4 (over y, core).
Axes of the slice: x: 2, y: 2, z: 4, core: 2. Of those that a mesh axis runs over, the one named last changes fastest.
Arguments:
- hidden_in: bfloat16 [8, 1088, 2048], P(('fsdp', 'replica'), 'ctx'), may hold values from -6 to 6
- memory_rows: bfloat16 [8, 50, 2048], P(('fsdp', 'replica')), may hold values from -6 to 6
- seg_len: int32 [8], P(('fsdp', 'replica')), may hold values from 519 to 1038, as said below
- out_grad: bfloat16 [8, 1088, 2048], P(('fsdp', 'replica'), 'ctx'), may hold values from -6 to 6
- first_gain: bfloat16 [2048], P('fsdp'), may hold values from 0.5 to 1.5
- first_shift: bfloat16 [2048], P('fsdp'), may hold values from -1 to 1
- qkv_weight: bfloat16 [2048, 6144], P('fsdp'), may hold values from -0.125 to 0.125
- query_bias: bfloat16 [2048], P('fsdp'), may hold values from -4 to 4
- value_bias: bfloat16 [2048], P('fsdp'), may hold values from -2.5 to 2.5
- out_weight: bfloat16 [2048, 2048], P('fsdp'), may hold values from -2 to 2
- out_bias: bfloat16 [2048], P('fsdp'), may hold values from -1 to 1
- second_gain: bfloat16 [2048], P('fsdp'), may hold values from 0.5 to 1.5
- second_shift: bfloat16 [2048], P('fsdp'), may hold values from -1 to 1
- up_weight: bfloat16 [2048, 8192], P('fsdp'), may hold values from -0.125 to 0.125
- up_bias: bfloat16 [8192], P('fsdp'), may hold values from -1 to 1
- down_weight: bfloat16 [8192, 2048], P('fsdp'), may hold values from -0.0625 to 0.0625
- down_bias: bfloat16 [2048], P('fsdp'), may hold values from -1 to 1
Outputs:
- output: bfloat16 [8, 1088, 2048], P(('fsdp', 'replica'), 'ctx')
- input_grad: float32 [8, 1088, 2048], P(('fsdp', 'replica'), 'ctx')
- memory_grad: float32 [8, 50, 2048], P(('fsdp', 'replica'))
- first_gain_grad: float32 [2048], P('fsdp')
- first_shift_grad: float32 [2048], P('fsdp')
- qkv_weight_grad: float32 [2048, 6144], P('fsdp')
- query_bias_grad: float32 [2048], P('fsdp')
- value_bias_grad: float32 [2048], P('fsdp')
- out_weight_grad: float32 [2048, 2048], P('fsdp')
- out_bias_grad: float32 [2048], P('fsdp')
- second_gain_grad: float32 [2048], P('fsdp')
- second_shift_grad: float32 [2048], P('fsdp')
- up_weight_grad: float32 [2048, 8192], P('fsdp')
- up_bias_grad: float32 [8192], P('fsdp')
- down_weight_grad: float32 [8192, 2048], P('fsdp')
- down_bias_grad: float32 [2048], P('fsdp')
The draws below stay inside these ranges and needn't reach their ends.
Inputs may be any that keep to these rules, and one draw needn't show every extreme that they name: Positions seg_len to 1037 of a segment are padding that no query uses as a key.
All inputs are finite; a program needn't handle non-finite values.
Results may differ from the reference program's by a relative error of at most 0.015.
Values may be sent and summed in bfloat16 or wider, within the bound.
No kernel may reach another device: no remote copies, remote signals or barrier semaphores. Data moves between devices by JAX's collectives and lax.ppermute only.
A program may use at most 512 MiB of HBM per device.

```python
import jax
import jax.numpy as jnp
from jax import lax

D = 2048
HEADS = 32
HEAD_DIM = 64
FF = 8192
SUMM = 50
SEQ_LEN = 1088
SEG = 1038
SEQS = 8


def draw_seg_len(key, part):
    first_key, second_key = jax.random.split(key)
    lengths = jax.random.randint(first_key, (SEQS,), SEG // 2, SEG + 1)
    chosen = jax.random.randint(second_key, (), 0, SEQS)
    return jnp.where(jnp.arange(SEQS) == chosen, SEG, lengths).astype(jnp.int32)


def block_scale(rng, dims, cuts, least, high):
    loudness, own = 1.0, jax.random.fold_in(rng, 6)
    for position, blocks in cuts:
        heights = jnp.exp(jax.random.uniform(jax.random.fold_in(own, position), (blocks,), jnp.float32, least / len(cuts), high / len(cuts)))
        loudness = loudness * jnp.repeat(heights, dims[position] // blocks).reshape([-1 if axis == position else 1 for axis in range(len(dims))])
    return loudness


def gaussian(key, dims, scale, reach, shards=(), kind=jnp.bfloat16):
    drawn = jax.random.normal(key, dims, jnp.float32) * scale
    if len(shards) > 0:
        drawn = block_scale(key, dims, shards, -0.22, 0.18) * drawn
    return jnp.clip(drawn, min=-reach, max=reach).astype(kind)


def setup_inputs(seed: int = 0) -> dict:
    splits = jax.random.split(jax.random.key(seed), 18)
    hidden_in = gaussian(splits[0], (SEQS, SEQ_LEN, D), 1.0, 6.0, ((0, 8), (1, 4)))
    memory_rows = gaussian(splits[1], (SEQS, SUMM, D), 1.0, 6.0, ((0, 8),))
    seg_len = draw_seg_len(jax.random.fold_in(splits[17], 71), 0)
    out_grad = gaussian(splits[3], (SEQS, SEQ_LEN, D), 1.0, 6.0, ((0, 8), (1, 4)))
    first_gain = jnp.clip(1.0 + 0.1 * jax.random.normal(splits[4], (D,), jnp.float32), 0.5, 1.5).astype(jnp.bfloat16)
    first_shift = gaussian(splits[5], (D,), 0.2, 1.0, ((0, 4),))
    qkv_weight = gaussian(splits[6], (D, 3 * D), D ** -0.5, 0.125, ((0, 4),))
    query_bias = gaussian(splits[7], (D,), 1.0, 4.0, ((0, 4),))
    value_bias = gaussian(splits[8], (D,), 0.5, 2.5, ((0, 4),))
    out_weight = gaussian(splits[9], (D, D), (max(D // 256, 1)) ** -0.5, 2.0, ((0, 4),))
    out_bias = gaussian(splits[10], (D,), 0.2, 1.0, ((0, 4),))
    second_gain = jnp.clip(1.0 + 0.1 * jax.random.normal(splits[11], (D,), jnp.float32), 0.5, 1.5).astype(jnp.bfloat16)
    second_shift = gaussian(splits[12], (D,), 0.2, 1.0, ((0, 4),))
    up_weight = gaussian(splits[13], (D, FF), D ** -0.5, 0.125, ((0, 4),))
    up_bias = gaussian(splits[14], (FF,), 0.2, 1.0, ((0, 4),))
    down_weight = gaussian(splits[15], (FF, D), FF ** -0.5, 0.0625, ((0, 4),))
    down_bias = gaussian(splits[16], (D,), 0.2, 1.0, ((0, 4),))
    return dict(hidden_in=hidden_in, memory_rows=memory_rows, seg_len=seg_len, out_grad=out_grad, first_gain=first_gain, first_shift=first_shift, qkv_weight=qkv_weight, query_bias=query_bias, value_bias=value_bias, out_weight=out_weight, out_bias=out_bias, second_gain=second_gain, second_shift=second_shift, up_weight=up_weight, up_bias=up_bias, down_weight=down_weight, down_bias=down_bias)


epsilon = 1e-05
highest = lax.Precision.HIGHEST
masked = -1e+30

@jax.custom_vjp
def low(v):
    return lax.optimization_barrier(v.astype(jnp.bfloat16)).astype(jnp.float32)

@jax.custom_vjp
def low_back(v):
    return v

def low_keep(v):
    return (low(v), None)

def low_pass(kept, grad):
    return (grad,)

def back_keep(v):
    return (v, None)

def back_low(kept, grad):
    return (low(grad),)
low.defvjp(low_keep, low_pass)
low_back.defvjp(back_keep, back_low)

def layer_norm(inputs, weight, offset):
    average = lax.optimization_barrier(jnp.mean(inputs, axis=-1, keepdims=True))
    centred = inputs - average
    spread = lax.optimization_barrier(jnp.mean(centred * centred, axis=-1, keepdims=True))
    return centred * lax.rsqrt(spread + epsilon) * weight + offset

def matmul(left, right):
    return jnp.dot(left, right, precision=highest)

def forward(params, hidden, memory, length):
    gain_one, shift_one, weight_qkv, bias_query, bias_value, weight_out, bias_out, gain_two, shift_two, weight_up, bias_up, weight_down, bias_down = params
    normed = low(layer_norm(hidden, gain_one, shift_one))
    mem_normed = low(layer_norm(memory, gain_one, shift_one))
    projected = matmul(normed, weight_qkv)
    mem_projected = matmul(mem_normed, weight_qkv[:, D:])
    query = low(low_back((projected[:, :D] + bias_query) * 0.125))
    keys = low(low_back(jnp.concatenate([mem_projected[:, :D], projected[:, D:2 * D]], axis=0)))
    values = low(low_back(jnp.concatenate([mem_projected[:, D:] + bias_value, projected[:, 2 * D:] + bias_value], axis=0)))
    places = jnp.arange(SEQ_LEN, dtype=jnp.int32)
    causal = places[None, :] <= places[:, None]
    present = (places < length) | (places >= SEG)
    allowed = jnp.concatenate([jnp.ones((SEQ_LEN, SUMM), dtype=bool), causal & present[None, :]], axis=1)
    query_heads = query.reshape(SEQ_LEN, HEADS, HEAD_DIM).transpose(1, 0, 2)
    key_heads = keys.reshape(SUMM + SEQ_LEN, HEADS, HEAD_DIM).transpose(1, 0, 2)
    value_heads = values.reshape(SUMM + SEQ_LEN, HEADS, HEAD_DIM).transpose(1, 0, 2)

    def one_head(operands):
        query_part, key_part, value_part = operands
        scores = low_back(jnp.dot(query_part, key_part.T, precision=highest))
        scores = jnp.where(allowed, scores, masked)
        largest = lax.optimization_barrier(jnp.max(scores, axis=-1, keepdims=True))
        expanded = jnp.exp(scores - largest)
        weights = expanded / lax.optimization_barrier(jnp.sum(expanded, axis=-1, keepdims=True))
        return jnp.dot(low(weights), value_part, precision=highest)
    mixed = lax.map(jax.checkpoint(one_head), (query_heads, key_heads, value_heads))
    attended = low(low_back(mixed.transpose(1, 0, 2).reshape(SEQ_LEN, D)))
    branch = low_back(matmul(attended, weight_out) + bias_out)
    middle = hidden + branch
    normed_two = low(layer_norm(middle, gain_two, shift_two))
    upper = low_back(matmul(normed_two, weight_up) + bias_up)
    active = low(jax.nn.gelu(upper, approximate=False))
    feed = low_back(matmul(active, weight_down) + bias_down)
    return middle + feed

def reference(hidden_in, memory_rows, seg_len, out_grad, first_gain, first_shift, qkv_weight, query_bias, value_bias, out_weight, out_bias, second_gain, second_shift, up_weight, up_bias, down_weight, down_bias):
    params = tuple((p_item.astype(jnp.float32) for p_item in (first_gain, first_shift, qkv_weight, query_bias, value_bias, out_weight, out_bias, second_gain, second_shift, up_weight, up_bias, down_weight, down_bias)))
    zeros = jax.tree.map(jnp.zeros_like, params)

    def step(carry, item):
        hidden, memory, length, cotangent = item

        def apply(param_set, hidden_f, memory_f):
            return forward(param_set, hidden_f, memory_f, length)
        result, pull = jax.vjp(apply, params, hidden.astype(jnp.float32), memory.astype(jnp.float32))
        grad_params, grad_hidden, grad_memory = pull(cotangent.astype(jnp.float32))
        carry = jax.tree.map(lambda left, right: left + right, carry, grad_params)
        return (carry, (result.astype(jnp.bfloat16), grad_hidden, grad_memory))
    totals, (output, input_grad, memory_grad) = lax.scan(step, zeros, (hidden_in, memory_rows, seg_len, out_grad))
    return (output, input_grad, memory_grad, totals[0], totals[1], totals[2], totals[3], totals[4], totals[5], totals[6], totals[7], totals[8], totals[9], totals[10], totals[11], totals[12])
```

```python
import jax
import jax.numpy as jnp
from jax import lax
from jax.sharding import PartitionSpec as P

D = 2048
HEADS = 32
HEAD_DIM = 64
SUMM = 50
SEQ_LEN = 1088
SEG = 1038
MEM_ROWS = 16

epsilon = 1e-05
masked = -1e30
f32 = jnp.float32
bf16 = jnp.bfloat16
PLANE = ("replica", "ctx")


def dot(left, right):
    return jnp.dot(left, right, preferred_element_type=f32)


def across(left, right):
    return lax.dot_general(left, right, (((0,), (0,)), ((), ())), preferred_element_type=f32)


def against(left, right):
    return lax.dot_general(left, right, (((1,), (1,)), ((), ())), preferred_element_type=f32)


def normal_of(rows):
    centred = rows - jnp.mean(rows, axis=-1, keepdims=True)
    inverse = lax.rsqrt(jnp.mean(centred * centred, axis=-1, keepdims=True) + epsilon)
    return centred * inverse, inverse


def norm_input_grad(upstream, normal, inverse, weight):
    scaled = upstream * weight
    centre = jnp.mean(scaled, axis=-1, keepdims=True)
    slope = jnp.mean(scaled * normal, axis=-1, keepdims=True)
    return inverse * (scaled - centre - normal * slope)


class Plane:
    def __init__(self):
        self.replicas = lax.axis_size("replica")
        self.spans = lax.axis_size("ctx")
        self.sizes = {"replica": self.replicas, "ctx": self.spans}
        self.slow = []
        bit = 1
        while bit < self.replicas:
            self.slow.append(("replica", bit))
            bit *= 2
        bit = 2
        while bit < self.spans:
            self.slow.append(("ctx", bit))
            bit *= 2
        self.fast = ("ctx", 1)
        spans = [v for v in range(self.spans) if v % 2 == 0] + [v for v in range(self.spans) if v % 2 == 1]
        self.span_order = spans
        self.order = [(r, v) for v in spans for r in range(self.replicas)]
        self.half = len(self.order) // 2

    def swap(self, array, stage):
        axis, bit = stage
        return lax.ppermute(array, axis, [(i, i ^ bit) for i in range(self.sizes[axis])])

    def step(self, name, stage):
        axis, bit = stage
        return (name[0] ^ bit, name[1]) if axis == "replica" else (name[0], name[1] ^ bit)

    def spread(self, rows):
        cut = cut_of(rows.shape[0])
        sides = [rows[:cut], rows[cut:]]
        found = [{(0, 0): sides[0]}, {(0, 0): sides[1]}]
        plans = [self.slow, self.slow[::-1]]
        for level in range(len(self.slow)):
            for side in range(2):
                stage = plans[side][level]
                for name, value in list(found[side].items()):
                    found[side][self.step(name, stage)] = self.swap(value, stage)
        pieces = []
        for name in self.order[: self.half]:
            pieces.append((found[0][name], found[1][name]))
        for upper, lower in list(pieces):
            pieces.append((self.swap(upper, self.fast), self.swap(lower, self.fast)))
        return pieces

    def gather(self, rows):
        return jnp.concatenate([half for piece in self.spread(rows) for half in piece], axis=0)

    def scatter(self, far, near):
        count = far.shape[0] // self.half
        cut = cut_of(count)
        names = self.order[: self.half]
        held = [{}, {}]
        for index in reversed(range(self.half)):
            sent = self.swap(far[index * count : (index + 1) * count], self.fast)
            kept = near[index * count : (index + 1) * count]
            total = kept.astype(f32) + sent.astype(f32)
            for side, part in enumerate((total[:cut], total[cut:])):
                held[side][names[index]] = part if index == 0 else part.astype(bf16)
        plans = [self.slow, self.slow[::-1]]
        for level in range(len(self.slow)):
            for side in range(2):
                stage = plans[side][level]
                later = plans[side][level + 1 :]
                kept = {}
                for name, value in held[side].items():
                    if self.bit(name, stage):
                        continue
                    moved = self.swap(held[side][self.step(name, stage)], stage)
                    total = value.astype(f32) + moved.astype(f32)
                    kept[name] = total if name == (0, 0) else total.astype(bf16)
                held[side] = kept
        return jnp.concatenate([held[0][(0, 0)], held[1][(0, 0)]], axis=0)

    def bit(self, name, stage):
        axis, bit = stage
        return (name[0] if axis == "replica" else name[1]) & bit


def cut_of(count):
    return (count // 2 + 15) // 16 * 16


def columns_of(weight, groups, index, width):
    span = weight.shape[1] // groups
    return jnp.concatenate(
        [lax.dynamic_slice_in_dim(weight, g * span + index * width, width, 1) for g in range(groups)], axis=1
    )


def allowed_of(plane, span_rows, own, lengths):
    places, slots = [], []
    for value in plane.span_order:
        base = own ^ value
        rows = jnp.arange(span_rows, dtype=jnp.int32) + base * span_rows
        mem = jnp.arange(MEM_ROWS, dtype=jnp.int32) + base * MEM_ROWS
        places.append((rows, mem))
    far = jnp.int32(1 << 30)
    queries = jnp.concatenate([rows for rows, _ in places])
    keys = jnp.concatenate([jnp.concatenate([rows, jnp.where(mem < SUMM, -1, far)]) for rows, mem in places])
    causal = keys[None, :] <= queries[:, None]
    present = (keys[None, :] < lengths[:, None]) | (keys[None, :] >= SEG)
    return causal[None] & present[:, None, :]


def attend(query, key, value, allowed):
    scores = jnp.einsum("gqhd,gkhd->ghqk", query, key, preferred_element_type=f32)
    scores = jnp.where(allowed[:, None], scores, masked)
    largest = jnp.max(scores, axis=-1, keepdims=True)
    expanded = jnp.exp(scores - largest)
    totals = jnp.sum(expanded, axis=-1, keepdims=True)
    weights = (expanded / totals).astype(bf16)
    mixed = jnp.einsum("ghqk,gkhd->gqhd", weights, value, preferred_element_type=f32)
    return mixed.astype(bf16), largest + jnp.log(totals)


def attend_back(query, key, value, upstream, log_totals, allowed):
    scores = jnp.einsum("gqhd,gkhd->ghqk", query, key, preferred_element_type=f32)
    scores = jnp.where(allowed[:, None], scores, masked)
    weights = jnp.exp(scores - log_totals)
    value_grad = jnp.einsum("ghqk,gqhd->gkhd", weights.astype(bf16), upstream, preferred_element_type=f32)
    weight_grad = jnp.einsum("gqhd,gkhd->ghqk", upstream, value, preferred_element_type=f32)
    centre = jnp.sum(weights * weight_grad, axis=-1, keepdims=True)
    score_grad = (weights * (weight_grad - centre)).astype(bf16)
    query_grad = jnp.einsum("ghqk,gkhd->gqhd", score_grad, key, preferred_element_type=f32)
    key_grad = jnp.einsum("ghqk,gqhd->gkhd", score_grad, query, preferred_element_type=f32)
    return query_grad.astype(bf16) * 0.125, key_grad.astype(bf16), value_grad.astype(bf16)


def shards(
    hidden_in,
    memory_rows,
    seg_len,
    out_grad,
    first_gain,
    first_shift,
    qkv_weight,
    query_bias,
    value_bias,
    out_weight,
    out_bias,
    second_gain,
    second_shift,
    up_weight,
    up_bias,
    down_weight,
    down_bias,
):
    plane = Plane()
    owners = lax.axis_size("fsdp")
    replicas, spans = plane.replicas, plane.spans
    team = replicas * spans
    pieces = len(plane.order)
    owner = lax.axis_index("fsdp")
    own_span = lax.axis_index("ctx")
    index = lax.axis_index("replica") * spans + own_span
    share = D // owners
    span_rows = hidden_in.shape[1]
    piece_rows = span_rows + MEM_ROWS
    heads = HEADS // team
    width = heads * HEAD_DIM
    hidden = up_bias.shape[0] // team
    ff = hidden * owners

    small = jnp.concatenate(
        [first_gain, first_shift, query_bias, value_bias, out_bias, second_gain, second_shift, down_bias, up_bias]
    )
    small = lax.all_gather(small.reshape(-1, 128), "fsdp", axis=0, tiled=True).reshape(owners, -1).astype(f32)
    vectors = [small[:, i * share : (i + 1) * share].reshape(D) for i in range(8)]
    gain_one, shift_one, bias_query, bias_value, bias_out, gain_two, shift_two, bias_down = vectors
    bias_up = lax.dynamic_slice_in_dim(small[:, 8 * share :], index * hidden, hidden, 1).reshape(ff)
    if heads % owners == 0:
        block = width // owners
        groups = owners
        weight_out = lax.all_gather(
            lax.dynamic_slice_in_dim(out_weight, index * block, block, 0), "fsdp", axis=0, tiled=True
        )
    else:
        block = width
        groups = 1
        weight_out = lax.dynamic_slice_in_dim(
            lax.all_gather(out_weight, "fsdp", axis=0, tiled=True), index * width, width, 0
        )
    weight_qkv = lax.all_gather(columns_of(qkv_weight, 3 * groups, index, block), "fsdp", axis=0, tiled=True)
    weight_up = lax.all_gather(columns_of(up_weight, owners, index, hidden), "fsdp", axis=0, tiled=True)
    weight_down = lax.all_gather(
        lax.dynamic_slice_in_dim(down_weight, index * hidden, hidden, 0), "fsdp", axis=0, tiled=True
    )
    my_bias = lambda vector: columns_of(vector[None], groups, index, block)[0]

    tokens = hidden_in.reshape(span_rows, D)
    slots = jnp.pad(memory_rows.reshape(SUMM, D), ((0, spans * MEM_ROWS - SUMM), (0, 0)))
    slots = lax.dynamic_slice_in_dim(slots, own_span * MEM_ROWS, MEM_ROWS, 0)
    own_rows = jnp.concatenate([tokens, slots], axis=0)
    all_rows = plane.gather(own_rows).astype(f32)
    normal_all, _ = normal_of(all_rows)
    normed = (normal_all * gain_one + shift_one).astype(bf16)
    bias_qkv = jnp.concatenate([my_bias(bias_query), jnp.zeros((width,), f32), my_bias(bias_value)])
    scale_qkv = jnp.concatenate([jnp.full((width,), 0.125, f32), jnp.ones((2 * width,), f32)])
    projected = ((dot(normed, weight_qkv) + bias_qkv) * scale_qkv).astype(bf16)

    lengths = [seg_len]
    for axis, bit in plane.slow:
        if axis == "replica":
            lengths = lengths + [plane.swap(v, (axis, bit)) for v in lengths]
    lengths = jnp.concatenate(lengths)

    def parts_of(array):
        array = array.reshape(spans, replicas, piece_rows, 3, heads, HEAD_DIM)
        array = jnp.moveaxis(array, 1, 0)
        query = array[:, :, :span_rows, 0].reshape(replicas, SEQ_LEN, heads, HEAD_DIM)
        key = array[:, :, :, 1].reshape(replicas, -1, heads, HEAD_DIM)
        value = array[:, :, :, 2].reshape(replicas, -1, heads, HEAD_DIM)
        return query, key, value

    query, key, value = parts_of(projected)
    allowed = allowed_of(plane, span_rows, own_span, lengths)
    mixed, log_totals = attend(query, key, value, allowed)
    to_pieces = lambda a: jnp.moveaxis(a.reshape(replicas, spans, -1, a.shape[-2] * a.shape[-1]), 0, 1)
    attended = to_pieces(mixed).reshape(pieces * span_rows, width)

    cut = plane.half * span_rows
    far = dot(attended[cut:], weight_out).astype(bf16)
    near = dot(attended[:cut], weight_out).astype(bf16)
    middle = tokens.astype(f32) + (plane.scatter(far, near) + bias_out)
    normal_two, inverse_two = normal_of(middle)
    normed_two = plane.gather((normal_two * gain_two + shift_two).astype(bf16))
    cotangent = out_grad.reshape(span_rows, D)
    cot_all = plane.gather(cotangent)

    upper = dot(normed_two, weight_up) + bias_up
    phi_up = 0.5 * (1.0 + lax.erf(upper * 0.7071067811865476))
    active = (upper * phi_up).astype(bf16)
    slope = phi_up + upper * (0.3989422804014327 * jnp.exp(-0.5 * upper * upper))
    upper_grad_f = against(cot_all, weight_down) * slope
    upper_grad = upper_grad_f.astype(bf16)
    far = against(upper_grad[cut:], weight_up).astype(bf16)
    near = against(upper_grad[:cut], weight_up).astype(bf16)
    normed_two_grad = plane.scatter(far, near)
    far = dot(active[cut:], weight_down).astype(bf16)
    near = dot(active[:cut], weight_down).astype(bf16)
    output = (middle + (plane.scatter(far, near) + bias_down)).astype(bf16)
    down_grad = across(active, cot_all).astype(bf16)
    up_grad = across(normed_two, upper_grad).astype(bf16)
    up_bias_grad = jnp.sum(upper_grad.astype(f32), axis=0)

    cot_float = cotangent.astype(f32)
    middle_grad = cot_float + norm_input_grad(normed_two_grad, normal_two, inverse_two, gain_two)
    branch_grad = middle_grad.astype(bf16)
    branch_all = plane.gather(branch_grad)
    mixed_grad = against(branch_all, weight_out).astype(bf16)
    out_grad_w = across(attended, branch_all).astype(bf16)
    upstream = jnp.moveaxis(mixed_grad.reshape(spans, replicas, span_rows, heads, HEAD_DIM), 1, 0)
    upstream = upstream.reshape(replicas, SEQ_LEN, heads, HEAD_DIM)
    query_grad, key_grad, value_grad = attend_back(query, key, value, upstream, log_totals, allowed)
    query_grad = jnp.pad(to_pieces(query_grad), ((0, 0), (0, 0), (0, MEM_ROWS), (0, 0)))
    projected_grad = jnp.concatenate([query_grad, to_pieces(key_grad), to_pieces(value_grad)], axis=-1)
    projected_grad = projected_grad.reshape(pieces * piece_rows, 3 * width)
    qkv_grad = across(normed, projected_grad).astype(bf16)
    qkv_bias_grad = jnp.sum(projected_grad.astype(f32), axis=0)
    cut = plane.half * piece_rows
    far = against(projected_grad[cut:], weight_qkv).astype(bf16)
    near = against(projected_grad[:cut], weight_qkv).astype(bf16)
    normed_grad = plane.scatter(far, near)
    normal_one, inverse_one = normal_of(own_rows.astype(f32))
    rows_grad = norm_input_grad(normed_grad, normal_one, inverse_one, gain_one)
    input_grad = middle_grad + rows_grad[:span_rows]
    slots_grad = lax.all_gather(rows_grad[span_rows:], "ctx", axis=0, tiled=True)[:SUMM]

    def settle(array, axis):
        mine = lax.psum_scatter(array, "fsdp", scatter_dimension=0, tiled=True)
        return lax.all_gather(mine, PLANE, axis=axis, tiled=False)

    down_all = settle(down_grad, 0).reshape(team * hidden, D).astype(f32)
    up_all = settle(up_grad, 0).reshape(team, share, owners, hidden)
    up_all = jnp.moveaxis(up_all, 0, 2).reshape(share, -1).astype(f32)
    qkv_all = settle(qkv_grad, 0).reshape(team, share, 3 * groups, block)
    qkv_all = jnp.moveaxis(qkv_all, 0, 2).reshape(share, 3 * D).astype(f32)
    if groups == owners:
        out_all = settle(out_grad_w, 0).reshape(share, D).astype(f32)
    else:
        placed = lax.dynamic_update_slice_in_dim(jnp.zeros((D, D), bf16), out_grad_w, index * width, 0)
        out_all = lax.psum(lax.psum_scatter(placed, "fsdp", scatter_dimension=0, tiled=True), PLANE).astype(f32)

    def spot(values, full, count, size):
        base = jnp.zeros((count, full // count), f32)
        return lax.dynamic_update_slice_in_dim(base, values.reshape(count, size), index * size, 1).reshape(full)

    totals = jnp.concatenate(
        [
            jnp.sum(normed_grad * normal_one, axis=0),
            jnp.sum(normed_grad, axis=0),
            spot(qkv_bias_grad[:width], D, groups, block),
            spot(qkv_bias_grad[2 * width :], D, groups, block),
            jnp.sum(branch_grad.astype(f32), axis=0),
            jnp.sum(normed_two_grad * normal_two, axis=0),
            jnp.sum(normed_two_grad, axis=0),
            jnp.sum(cot_float, axis=0),
            spot(up_bias_grad, ff * team, owners, hidden),
        ]
    )
    totals = lax.psum(totals, ("fsdp", "replica", "ctx"))
    take = lambda i: lax.dynamic_slice_in_dim(totals, i * D + owner * share, share)
    up_share = ff * team // owners
    return (
        output.reshape(hidden_in.shape),
        input_grad.reshape(hidden_in.shape),
        slots_grad.reshape(memory_rows.shape),
        take(0),
        take(1),
        qkv_all,
        take(2),
        take(3),
        out_all,
        take(4),
        take(5),
        take(6),
        up_all,
        lax.dynamic_slice_in_dim(totals, 8 * D + owner * up_share, up_share),
        down_all,
        take(7),
    )


def solution(mesh):
    rows = P(("fsdp", "replica"), "ctx", None)
    part = P("fsdp")
    table = P("fsdp", None)
    whole = P(("fsdp", "replica"), None, None)
    return jax.shard_map(
        shards,
        mesh=mesh,
        in_specs=(
            rows,
            whole,
            P(("fsdp", "replica")),
            rows,
            part,
            part,
            table,
            part,
            part,
            table,
            part,
            part,
            part,
            table,
            part,
            table,
            part,
        ),
        out_specs=(
            rows,
            rows,
            whole,
            part,
            part,
            table,
            part,
            part,
            table,
            part,
            part,
            part,
            table,
            part,
            table,
            part,
        ),
        check_vma=False,
    )
```

```python
import functools

import jax
import jax.numpy as jnp
import numpy as np
from jax import lax
from jax.experimental import pallas as pl
from jax.experimental.pallas import tpu as pltpu
from jax.sharding import PartitionSpec as P

D = 2048
HEADS = 32
HEAD_DIM = 64
SUMM = 50
SEQ_LEN = 1088
SEG = 1038
MEM_ROWS = 16
LANES = 128
QUERY_BLOCK = 256
ROW_BLOCK = 64

epsilon = 1e-05
masked = -1e30
f32 = jnp.float32
bf16 = jnp.bfloat16
PLANE = ("replica", "ctx")


def dot(left, right):
    return jnp.dot(left, right, preferred_element_type=f32)


def across(left, right):
    return lax.dot_general(left, right, (((0,), (0,)), ((), ())), preferred_element_type=f32)


def against(left, right):
    return lax.dot_general(left, right, (((1,), (1,)), ((), ())), preferred_element_type=f32)


def normal_of(rows):
    centred = rows - jnp.mean(rows, axis=-1, keepdims=True)
    inverse = lax.rsqrt(jnp.mean(centred * centred, axis=-1, keepdims=True) + epsilon)
    return centred * inverse, inverse


def norm_input_grad(upstream, normal, inverse, weight):
    scaled = upstream * weight
    centre = jnp.mean(scaled, axis=-1, keepdims=True)
    slope = jnp.mean(scaled * normal, axis=-1, keepdims=True)
    return inverse * (scaled - centre - normal * slope)


class Plane:
    def __init__(self):
        self.replicas = lax.axis_size("replica")
        self.spans = lax.axis_size("ctx")
        self.sizes = {"replica": self.replicas, "ctx": self.spans}
        self.slow = []
        for axis, bit in (("replica", 1), ("ctx", 2)):
            while bit < self.sizes[axis]:
                self.slow.append((axis, bit))
                bit *= 2
        self.fast = ("ctx", 1)
        self.near = [(r, v) for v in range(0, self.spans, 2) for r in range(self.replicas)]
        self.far = [(r, v + 1) for r, v in self.near]
        self.half = len(self.near)

    def swap(self, array, stage=None):
        axis, bit = stage or self.fast
        return lax.ppermute(array, axis, [(i, i ^ bit) for i in range(self.sizes[axis])])

    def step(self, name, stage):
        axis, bit = stage
        return (name[0] ^ bit, name[1]) if axis == "replica" else (name[0], name[1] ^ bit)

    def bit(self, name, stage):
        axis, bit = stage
        return (name[0] if axis == "replica" else name[1]) & bit

    def send(self, rows, cut=None):
        cut = cut or cut_of(rows.shape[0])
        sides = [rows[:cut], rows[cut:]]
        return [[self.swap(side, stage) for stage in plan] for side, plan in zip(sides, (self.slow, self.slow[::-1]))]

    def travel(self, rows, fills=(), cut=None, first=None):
        cut = cut or cut_of(rows.shape[0])
        plans = [self.slow, self.slow[::-1]]
        found = [{(0, 0): rows[:cut]}, {(0, 0): rows[cut:]}]
        first = first or self.send(rows, cut)
        results = []
        for level in range(len(self.slow)):
            arrived = []
            for side in range(2):
                stage = plans[side][level]
                for name, value in list(found[side].items()):
                    moved = first[side][level] if name == (0, 0) else self.swap(value, stage)
                    name = self.step(name, stage)
                    found[side][name] = moved
                    if level == 0 or name != self.step((0, 0), stage):
                        arrived.append((side, name))
            if level < len(fills) and fills[level] is not None:
                filled = fills[level]()
                side, name = arrived[-1]
                found[side][name], filled = lax.optimization_barrier((found[side][name], filled))
                results.append(filled)
        return found, results

    def gather(self, rows, fills=(), first=None):
        found, results = self.travel(rows, fills, None, first)
        return jnp.concatenate([found[side][name] for name in self.near for side in range(2)], axis=0), results

    def sides(self, found):
        sides = [[found[side][name] for name in self.near] for side in range(2)]
        return [side + [self.swap(value) for value in side] for side in sides]

    def spread(self, block, cut=None, first=None):
        return self.sides(self.travel(block, (), cut, first)[0])

    def scatter(self, partial, fills=(), before=()):
        count = partial.shape[0] // self.half
        cut = cut_of(count)
        held = [{}, {}]
        for index, name in enumerate(self.near):
            held[0][name] = partial[index * count : index * count + cut]
            held[1][name] = partial[index * count + cut : (index + 1) * count]
        plans = [self.slow, self.slow[::-1]]
        results = []
        for level in range(len(self.slow)):
            moves = []
            for side in range(2):
                stage = plans[side][level]
                for name in reversed(held[side]):
                    if not self.bit(name, stage):
                        moves.append((side, name, held[side][self.step(name, stage)], stage))
            filled = None
            if level < len(fills):
                filled = fills[level](moves[-1][2])
            if before and level == 0:
                moves = [(*move[:2], gate([move[2]], *before)[0], move[3]) if move[1] != (0, 0) else move for move in moves]
            kept = [{}, {}]
            for number, (side, name, value, stage) in enumerate(moves):
                moved = self.swap(value, stage)
                if filled is not None and number == len(moves) - 1:
                    moved, filled = lax.optimization_barrier((moved, filled))
                    results.append(filled)
                total = held[side][name].astype(f32) + moved.astype(f32)
                kept[side][name] = total if name == (0, 0) else total.astype(bf16)
            held = kept
        for fill in fills[len(self.slow) :]:
            results.append(fill(held[0][(0, 0)]))
        return jnp.concatenate([held[0][(0, 0)], held[1][(0, 0)]], axis=0), results

    def whole(self, block):
        found = {(0, 0): block}
        firsts = [self.step((0, 0), stage) for stage in self.slow]
        for name, stage in zip(firsts, self.slow):
            found[name] = self.swap(block, stage)
        return found

    def complete(self, found, turned, before=()):
        if before:
            names = [name for name in found if name != (0, 0)]
            held = gate([found[name] for name in names], *before)
            found = {(0, 0): found[(0, 0)], **dict(zip(names, held))}
        for stage in self.slow[::-1] if turned else self.slow:
            for name, value in list(found.items()):
                name = self.step(name, stage)
                if name not in found:
                    found[name] = self.swap(value, stage)
        near = [found[name] for name in self.near]
        return [near + [self.swap(value) for value in near]]


def cut_of(count):
    return (count // 2 + 15) // 16 * 16


def columns_of(weight, groups, index, width, order=None):
    span = weight.shape[1] // groups
    order = range(groups) if order is None else order
    return jnp.concatenate(
        [lax.dynamic_slice_in_dim(weight, g * span + index * width, width, 1) for g in order], axis=1
    )


def allowed_of(plane, span_rows, own, lengths):
    places, slots = [], []
    for value in [v for _, v in plane.near + plane.far if _ == 0]:
        base = own ^ value
        rows = jnp.arange(span_rows, dtype=jnp.int32) + base * span_rows
        mem = jnp.arange(MEM_ROWS, dtype=jnp.int32) + base * MEM_ROWS
        places.append((rows, mem))
    far = jnp.int32(1 << 30)
    queries = jnp.concatenate([rows for rows, _ in places])
    keys = jnp.concatenate([jnp.concatenate([rows, jnp.where(mem < SUMM, -1, far)]) for rows, mem in places])
    causal = keys[None, :] <= queries[:, None]
    present = (keys[None, :] < lengths[:, None]) | (keys[None, :] >= SEG)
    return causal[None] & present[:, None, :]


def attend(query, key, value, allowed):
    scores = jnp.einsum("gqhd,gkhd->ghqk", query, key, preferred_element_type=f32)
    scores = jnp.where(allowed[:, None], scores, masked)
    largest = jnp.max(scores, axis=-1, keepdims=True)
    expanded = jnp.exp(scores - largest)
    totals = jnp.sum(expanded, axis=-1, keepdims=True)
    weights = (expanded / totals).astype(bf16)
    mixed = jnp.einsum("ghqk,gkhd->gqhd", weights, value, preferred_element_type=f32)
    return mixed.astype(bf16), largest + jnp.log(totals)


def attend_back(query, key, value, upstream, log_totals, allowed):
    scores = jnp.einsum("gqhd,gkhd->ghqk", query, key, preferred_element_type=f32)
    scores = jnp.where(allowed[:, None], scores, masked)
    weights = jnp.exp(scores - log_totals)
    value_grad = jnp.einsum("ghqk,gqhd->gkhd", weights.astype(bf16), upstream, preferred_element_type=f32)
    weight_grad = jnp.einsum("gqhd,gkhd->ghqk", upstream, value, preferred_element_type=f32)
    centre = jnp.sum(weights * weight_grad, axis=-1, keepdims=True)
    score_grad = (weights * (weight_grad - centre)).astype(bf16)
    query_grad = jnp.einsum("ghqk,gkhd->gqhd", score_grad, key, preferred_element_type=f32)
    key_grad = jnp.einsum("ghqk,gqhd->gkhd", score_grad, query, preferred_element_type=f32)
    return query_grad.astype(bf16) * 0.125, key_grad.astype(bf16), value_grad.astype(bf16)


def blocks_of(count):
    starts = list(range(0, count, QUERY_BLOCK))
    return [(s, min(QUERY_BLOCK, count - s)) for s in starts]


def piece_of(own, c):
    v = jnp.bitwise_xor(own, c)
    return jnp.right_shift(v, 1), jnp.bitwise_and(v, 1) == 0


def to_sequence(spans, span_rows, own, near, far, target, with_slots=True):
    base = spans * MEM_ROWS
    for c in range(spans):
        slot, is_near = piece_of(own, c)
        rows = jnp.where(is_near, near[slot, 0, :span_rows, :], far[slot, 0, :span_rows, :])
        target[base + c * span_rows : base + (c + 1) * span_rows] = rows
        if with_slots:
            rows = jnp.where(is_near, near[slot, 0, span_rows:, :], far[slot, 0, span_rows:, :])
            target[c * MEM_ROWS : (c + 1) * MEM_ROWS] = rows
    if not with_slots:
        target[:base] = jnp.zeros((base, target.shape[1]), target.dtype)


def key_bias(length, spans, seq_len):
    base = spans * MEM_ROWS
    shape = (base + seq_len, LANES)
    row = lax.broadcasted_iota(jnp.int32, shape, 0)
    place = row - base
    good = (row < SUMM) | ((place >= 0) & ((place < length) | (place >= SEG)))
    return jnp.where(good, 0.0, masked).astype(f32)


def head_masks(count):
    lane = lax.broadcasted_iota(jnp.int32, (count, LANES), 1)
    return lane < HEAD_DIM, lane == HEAD_DIM, lane == 0


def headed(array, masks, head):
    return jnp.where(masks[0] if head == 0 else ~masks[0], array, 0.0)


def scores_of(keys, query, start, size, base):
    stop = start + size
    scores = against(keys[:stop], query[start:stop])
    tail = scores[start:stop]
    row = lax.broadcasted_iota(jnp.int32, (size, size), 0)
    column = lax.broadcasted_iota(jnp.int32, (size, size), 1)
    seen = row <= column
    if start < base:
        seen = seen | (row < base - start)
    tail = jnp.where(seen, tail, masked)
    return tail if start == 0 else jnp.concatenate([scores[:start], tail], axis=0)


def attend_kernel(spans, span_rows, info, qn, qf, kn, kf, vn, vf, on, of, lse_ref, q_all, k_all, v_all, o_all):
    count = k_all.shape[0]
    base = spans * MEM_ROWS
    own = info[0]
    to_sequence(spans, span_rows, own, qn, qf, q_all)
    to_sequence(spans, span_rows, own, kn, kf, k_all)
    to_sequence(spans, span_rows, own, vn, vf, v_all)
    masks = head_masks(count)
    bias = key_bias(info[1 + pl.program_id(0)], spans, count - base)
    query, key = q_all[...].astype(f32), k_all[...].astype(f32)
    values = v_all[...].astype(f32).T.astype(bf16)
    queries, keys = [], []
    for head in range(2):
        flag = masks[1] if head == 0 else masks[2]
        queries.append((headed(query, masks, head) + jnp.where(flag, 1.0, 0.0)).astype(bf16))
        keys.append((headed(key, masks, head) + jnp.where(flag, bias, 0.0)).astype(bf16))
    for start, size in blocks_of(count):
        tops = []
        for head in range(2):
            scores = scores_of(keys[head], queries[head], start, size, base)
            largest = jnp.max(scores, axis=0, keepdims=True)
            expanded = jnp.exp(scores - largest)
            totals = jnp.sum(expanded, axis=0, keepdims=True)
            lse_ref[0, 0, head : head + 1, start : start + size] = largest + jnp.log(totals)
            mixed = jnp.dot(values[:, : start + size], expanded.astype(bf16), preferred_element_type=f32)
            tops.append(mixed[head * HEAD_DIM : (head + 1) * HEAD_DIM] / totals)
        o_all[start : start + size] = jnp.concatenate(tops, axis=0).T.astype(bf16)
    for c in range(spans):
        slot, is_near = piece_of(own, c)
        for target, chosen in ((on, is_near), (of, jnp.logical_not(is_near))):

            @pl.when(chosen)
            def _(c=c, slot=slot, target=target):
                target[slot, 0] = o_all[base + c * span_rows : base + (c + 1) * span_rows]


def attend_back_kernel(spans, span_rows, info, qn, qf, kn, kf, vn, vf, on, of, gn, gf, lse_ref, *rest):
    d_near, d_far, q_all, k_all, v_all, o_all, g_all, dq, dk, dv = rest[-10:]
    count = k_all.shape[0]
    base = spans * MEM_ROWS
    own = info[0]
    to_sequence(spans, span_rows, own, qn, qf, q_all)
    to_sequence(spans, span_rows, own, kn, kf, k_all)
    to_sequence(spans, span_rows, own, vn, vf, v_all)
    to_sequence(spans, span_rows, own, on, of, o_all, False)
    to_sequence(spans, span_rows, own, gn, gf, g_all, False)
    masks = head_masks(count)
    bias = key_bias(info[1 + pl.program_id(0)], spans, count - base)
    query, key, grad = q_all[...].astype(f32), k_all[...].astype(f32), g_all[...].astype(f32)
    overlap = (grad * o_all[...].astype(f32)).T
    keys_t = key.T.astype(bf16)
    values = v_all[...]
    plain_q, plain_g, flag_q, flag_k, deltas = [], [], [], [], []
    for head in range(2):
        flag = masks[1] if head == 0 else masks[2]
        own_q = headed(query, masks, head)
        plain_q.append(own_q.astype(bf16))
        plain_g.append(headed(grad, masks, head).astype(bf16))
        flag_q.append((own_q + jnp.where(flag, 1.0, 0.0)).astype(bf16))
        flag_k.append((headed(key, masks, head) + jnp.where(flag, bias, 0.0)).astype(bf16))
        deltas.append(jnp.sum(overlap[head * HEAD_DIM : (head + 1) * HEAD_DIM], axis=0, keepdims=True))
    for start, size in reversed(blocks_of(count)):
        stop = start + size
        tops, weights_low, slopes = [], [], []
        for head in range(2):
            scores = scores_of(flag_k[head], flag_q[head], start, size, base)
            weights = jnp.exp(scores - lse_ref[0, 0, head : head + 1, start:stop])
            weight_grad = against(values[:stop], plain_g[head][start:stop])
            slope = (weights * (weight_grad - deltas[head][:, start:stop])).astype(bf16)
            weights_low.append(weights.astype(bf16))
            slopes.append(slope)
            turned = jnp.dot(keys_t[:, :stop], slope, preferred_element_type=f32)
            tops.append(turned[head * HEAD_DIM : (head + 1) * HEAD_DIM])
        dq[start:stop] = (jnp.concatenate(tops, axis=0).T.astype(bf16).astype(f32) * 0.125).astype(bf16)
        grads = jnp.concatenate([plain_g[0][start:stop], plain_g[1][start:stop]], axis=0)
        queries = jnp.concatenate([plain_q[0][start:stop], plain_q[1][start:stop]], axis=0)
        value_part = jnp.dot(jnp.concatenate(weights_low, axis=1), grads, preferred_element_type=f32)
        key_part = jnp.dot(jnp.concatenate(slopes, axis=1), queries, preferred_element_type=f32)
        if stop == count:
            dv[...] = value_part
            dk[...] = key_part
        else:
            dv[:stop] += value_part
            dk[:stop] += key_part
    for c in range(spans):
        slot, is_near = piece_of(own, c)
        rows = slice(base + c * span_rows, base + (c + 1) * span_rows)
        slots = slice(c * MEM_ROWS, (c + 1) * MEM_ROWS)
        for target, chosen in ((d_near, is_near), (d_far, jnp.logical_not(is_near))):

            @pl.when(chosen)
            def _(slot=slot, rows=rows, slots=slots, target=target):
                for part, source in enumerate((dq, dk, dv)):
                    lanes = slice(part * LANES, (part + 1) * LANES)
                    target[slot, 0, :span_rows, lanes] = source[rows].astype(bf16)
                    low = jnp.zeros((MEM_ROWS, LANES), bf16) if part == 0 else source[slots].astype(bf16)
                    target[slot, 0, span_rows:, lanes] = low


def attend_call(info, near, far, span_rows, heads):
    slots, replicas, rows, _ = near.shape
    spans, pairs = 2 * slots, heads // 2
    count = spans * rows
    piece = lambda part: [pl.BlockSpec((slots, 1, rows, LANES), lambda r, p, info: (0, r, 0, 3 * p + part))] * 2
    mixed = pl.BlockSpec((slots, 1, span_rows, LANES), lambda r, p, info: (0, r, 0, p))
    shape = jax.ShapeDtypeStruct((slots, replicas, span_rows, pairs * LANES), bf16)
    return pl.pallas_call(
        functools.partial(attend_kernel, spans, span_rows),
        out_shape=(shape, shape, jax.ShapeDtypeStruct((replicas, pairs, 2, count), f32)),
        grid_spec=pltpu.PrefetchScalarGridSpec(
            num_scalar_prefetch=1,
            grid=(replicas, pairs),
            in_specs=piece(0) + piece(1) + piece(2),
            out_specs=(mixed, mixed, pl.BlockSpec((1, 1, 2, count), lambda r, p, info: (r, p, 0, 0))),
            scratch_shapes=[pltpu.VMEM((count, LANES), bf16)] * 4,
        ),
        compiler_params=pltpu.CompilerParams(vmem_limit_bytes=56 << 20),
        cost_estimate=pl.CostEstimate(flops=24 * 10**9, bytes_accessed=8 * 10**6, transcendentals=10**7),
        name="attend",
    )(info, near, far, near, far, near, far)


def attend_back_call(info, projected, attended, upstream, log_totals, span_rows, heads):
    slots, replicas, rows, _ = projected[0].shape
    spans, pairs = 2 * slots, heads // 2
    count = spans * rows
    piece = lambda part: [pl.BlockSpec((slots, 1, rows, LANES), lambda r, p, info: (0, r, 0, 3 * p + part))] * 2
    plain = [pl.BlockSpec((slots, 1, span_rows, LANES), lambda r, p, info: (0, r, 0, p))] * 4
    specs = piece(0) + piece(1) + piece(2) + plain
    specs.append(pl.BlockSpec((1, 1, 2, count), lambda r, p, info: (r, p, 0, 0)))
    inputs = [*projected, *projected, *projected, *attended, *upstream, log_totals]
    shape = jax.ShapeDtypeStruct((slots, replicas, rows, 3 * pairs * LANES), bf16)
    return pl.pallas_call(
        functools.partial(attend_back_kernel, spans, span_rows),
        out_shape=(shape, shape),
        grid_spec=pltpu.PrefetchScalarGridSpec(
            num_scalar_prefetch=1,
            grid=(replicas, pairs),
            in_specs=specs,
            out_specs=[pl.BlockSpec((slots, 1, rows, 3 * LANES), lambda r, p, info: (0, r, 0, p))] * 2,
            scratch_shapes=[pltpu.VMEM((count, LANES), bf16)] * 6 + [pltpu.VMEM((count, LANES), f32)] * 2,
        ),
        compiler_params=pltpu.CompilerParams(vmem_limit_bytes=56 << 20),
        cost_estimate=pl.CostEstimate(flops=30 * 10**9, bytes_accessed=16 * 10**6, transcendentals=10**7),
        name="attend_back",
    )(info, *inputs)


def place_up_kernel(owners, table, *refs):
    target = refs[-1]
    width = refs[0].shape[1] // owners
    team = target.shape[1] // (owners * width)
    for k in range(team):
        for z in range(owners):
            lanes = pl.ds(pl.multiple_of((z * team + table[k]) * width, width), width)
            target[:, lanes] = refs[k][:, z * width : (z + 1) * width].astype(f32)


def place_heads_kernel(order, table, *refs):
    target = refs[-1]
    groups = len(order)
    width = refs[0].shape[1] // groups
    team = target.shape[1] // (groups * width)
    half = team // 2
    odd = table[0] % 2 == 1
    for k in range(half):
        mine, other = refs[k][...].astype(f32), refs[k + half][...].astype(f32)
        first = jnp.where(odd, other, mine)
        second = jnp.where(odd, mine, other)
        place = table[k] // 2
        for position, g in enumerate(order):
            cut = slice(position * width, (position + 1) * width)
            lanes = pl.ds(pl.multiple_of((g * half + place) * 2 * width, 2 * width), 2 * width)
            target[:, lanes] = jnp.concatenate([first[:, cut], second[:, cut]], axis=1)


def place_columns(kernel, table, sides, rows, columns):
    result = None
    size = rows // len(sides)
    for number, side in enumerate(sides):
        inputs = list(side)
        if side[0].ndim == 3:
            block = (None, ROW_BLOCK, side[0].shape[2])
            specs = [pl.BlockSpec(block, lambda i, t, k=k: (k, i, 0)) for k in range(len(side))]
        else:
            specs = [pl.BlockSpec((ROW_BLOCK, side[0].shape[1]), lambda i, t: (i, 0))] * len(side)
        shift = number * size // ROW_BLOCK
        result = placed(kernel, table, inputs, specs, result, (rows, columns), (ROW_BLOCK, columns), size // ROW_BLOCK, lambda i, t: (i + shift, 0))
    return result


def placed(kernel, table, inputs, specs, result, shape, block, steps, index):
    aliases = {}
    if result is not None:
        inputs.append(result)
        specs.append(pl.BlockSpec(memory_space=pl.ANY))
        aliases = {len(inputs): 0}
    return pl.pallas_call(
        kernel,
        out_shape=jax.ShapeDtypeStruct(shape, f32),
        grid_spec=pltpu.PrefetchScalarGridSpec(
            num_scalar_prefetch=1,
            grid=(steps,),
            in_specs=specs,
            out_specs=pl.BlockSpec(block, index),
        ),
        input_output_aliases=aliases,
        compiler_params=pltpu.CompilerParams(vmem_limit_bytes=40 << 20),
        cost_estimate=pl.CostEstimate(flops=0, bytes_accessed=6 * steps * block[0] * block[1], transcendentals=0),
        name="place",
    )(table, *inputs)


def place_rows_kernel(team, table, *refs):
    target = refs[-1]
    for k in range(team):

        @pl.when(pl.program_id(0) == k)
        def _(k=k):
            target[...] = refs[k][...].astype(f32)


def place_rows(table, sides, used=None):
    team = len(sides[0])
    result = None
    count = len(sides)
    for number, side in enumerate(sides):
        size, columns = (used or side[0].shape[0]), side[0].shape[1]
        specs = [pl.BlockSpec((size, columns), lambda i, t: (0, 0), pipeline_mode=pl.Buffered(1))] * team
        kernel = functools.partial(place_rows_kernel, team)
        shape = (count * size * team, columns)
        result = placed(kernel, table, list(side), specs, result, shape, (size, columns), team, lambda i, t, number=number: (count * t[i] + number, 0))
    return result


def hold(value, *others):
    return lax.optimization_barrier((value, *others))[0]


def gate(values, *others):
    values = list(values)
    anywhere = pl.BlockSpec(memory_space=pl.ANY)
    return pl.pallas_call(
        lambda *refs: None,
        out_shape=[jax.ShapeDtypeStruct(v.shape, v.dtype) for v in values],
        in_specs=[anywhere] * (len(values) + len(others)),
        out_specs=[anywhere] * len(values),
        input_output_aliases={i: i for i in range(len(values))},
        name="gate",
    )(*values, *others)


def shards(
    hidden_in,
    memory_rows,
    seg_len,
    out_grad,
    first_gain,
    first_shift,
    qkv_weight,
    query_bias,
    value_bias,
    out_weight,
    out_bias,
    second_gain,
    second_shift,
    up_weight,
    up_bias,
    down_weight,
    down_bias,
):
    plane = Plane()
    owners = lax.axis_size("fsdp")
    replicas, spans = plane.replicas, plane.spans
    team = replicas * spans
    count = plane.half
    owner = lax.axis_index("fsdp")
    own_span = lax.axis_index("ctx")
    index = lax.axis_index("replica") * spans + own_span
    mate = jnp.bitwise_xor(index, 1)
    share = D // owners
    span_rows = hidden_in.shape[1]
    piece_rows = span_rows + MEM_ROWS
    heads = HEADS // team
    width = heads * HEAD_DIM
    hidden = up_bias.shape[0] // team
    ff = hidden * owners
    low = lambda array: array.astype(bf16)

    even = heads % owners == 0
    block = width // owners if even else width
    groups = owners if even else 1
    pairs = max(heads // 2, 1)
    inner = groups // pairs if groups > 1 else 1
    order = [part * groups + pair * inner + i for pair in range(pairs) for part in range(3) for i in range(inner)]
    columns_qkv = columns_of(qkv_weight, 3 * groups, index, block, order)
    weight_qkv = lax.all_gather(columns_qkv, "fsdp", axis=0, tiled=True)
    small = jnp.concatenate(
        [first_gain, first_shift, query_bias, value_bias, out_bias, second_gain, second_shift, down_bias, up_bias]
    )
    small = lax.all_gather(hold(small, columns_qkv).reshape(-1, 128), "fsdp", axis=0, tiled=True)
    small = small.reshape(owners, -1).astype(f32)
    vectors = [small[:, i * share : (i + 1) * share].reshape(D) for i in range(8)]
    gain_one, shift_one, bias_query, bias_value, bias_out, gain_two, shift_two, bias_down = vectors
    bias_up = jnp.concatenate(
        [lax.dynamic_slice_in_dim(small[:, 8 * share :], i * hidden, hidden, 1).reshape(ff) for i in (index, mate)]
    )
    if even:
        rows_out = lax.dynamic_slice_in_dim(out_weight, index * block, block, 0)
        weight_out = lax.all_gather(rows_out, "fsdp", axis=0, tiled=True)
    else:
        weight_out = lax.dynamic_slice_in_dim(
            lax.all_gather(out_weight, "fsdp", axis=0, tiled=True), index * width, width, 0
        )
    weight_up = lax.all_gather(columns_of(up_weight, owners, index, hidden), "fsdp", axis=0, tiled=True)
    weight_down = lax.all_gather(
        lax.dynamic_slice_in_dim(down_weight, index * hidden, hidden, 0), "fsdp", axis=0, tiled=True
    )
    with_mate = lambda weight, axis: jnp.concatenate([weight, plane.swap(weight)], axis=axis)

    cotangent = out_grad.reshape(span_rows, D)
    cot_float = cotangent.astype(f32)
    cot_first = plane.send(cotangent)

    tokens = hold(hidden_in, cot_first).reshape(span_rows, D)
    slots = jnp.pad(memory_rows.reshape(SUMM, D), ((0, spans * MEM_ROWS - SUMM), (0, 0)))
    slots = lax.dynamic_slice_in_dim(slots, own_span * MEM_ROWS, MEM_ROWS, 0)
    own_rows = jnp.concatenate([tokens, slots], axis=0).astype(f32)
    normal_one, inverse_one = normal_of(own_rows)
    lengths = [seg_len]
    for axis, bit in plane.slow:
        if axis == "replica":
            lengths = lengths + [plane.swap(v, (axis, bit)) for v in lengths]
    lengths = jnp.concatenate(lengths)

    normed, _ = plane.gather(hold(low(normal_one * gain_one + shift_one), lengths))
    weight_qkv = hold(weight_qkv, normed)
    qkv_mate = plane.swap(weight_qkv)
    bias_qkv = jnp.concatenate([bias_query, jnp.zeros((D,), f32), bias_value])[None]
    scale_qkv = jnp.asarray(np.repeat([0.125 if g < groups else 1.0 for g in order], block), f32)

    def project(rows, weight, device):
        bias = columns_of(bias_qkv, 3 * groups, device, block, order)[0]
        return low((dot(rows, weight) + bias) * scale_qkv).reshape(spans // 2, replicas, piece_rows, 3 * width)

    kernels = span_rows % 16 == 0 and heads % 2 == 0 and spans % 2 == 0 and SUMM <= spans * MEM_ROWS
    info = jnp.concatenate([own_span[None].astype(jnp.int32), lengths])
    split = lambda a: jnp.moveaxis(a, 1, 0).reshape(replicas, -1, heads, HEAD_DIM)
    to_pieces = lambda a: jnp.moveaxis(a.reshape(replicas, spans, -1, pairs, width // pairs), 0, 1)

    def parts_of(near, far):
        apart = jnp.concatenate([near, far], axis=0).reshape(spans, replicas, piece_rows, pairs, 3, width // pairs)
        return split(apart[:, :, :span_rows, :, 0]), split(apart[..., 1, :]), split(apart[..., 2, :])

    def attend_all():
        near, far = projected
        if kernels:
            return attend_call(info, near, far, span_rows, heads)
        allowed = allowed_of(plane, span_rows, own_span, lengths)
        mixed, totals = attend(*parts_of(near, far), allowed)
        mixed = to_pieces(mixed).reshape(spans, replicas, span_rows, width)
        return mixed[: spans // 2], mixed[spans // 2 :], totals

    projected = [project(normed, weight_qkv, index)]
    projected.append(plane.swap(project(normed, hold(qkv_mate, projected[0]), mate)))
    cot_all, filled = plane.gather(cotangent, (None, attend_all), cot_first)
    mixed_near, mixed_far, log_totals = filled[0]
    attended = jnp.concatenate([mixed_near, plane.swap(mixed_far)], axis=-1).reshape(count * span_rows, 2 * width)
    weight_out = with_mate(hold(weight_out, projected[0]), 0)
    branch, _ = plane.scatter(low(dot(attended, weight_out)))
    bias_out = gate([bias_out[None]], cot_all)[0][0] if kernels else bias_out
    weight_up = with_mate(gate([weight_up], branch)[0] if kernels else weight_up, 1)
    middle = tokens.astype(f32) + (branch + bias_out)
    normal_two, inverse_two = normal_of(middle)
    normed_two, _ = plane.gather(low(normal_two * gain_two + shift_two))

    upper = dot(normed_two, weight_up) + bias_up
    phi_up = 0.5 * (1.0 + lax.erf(upper * 0.7071067811865476))
    active = low(upper * phi_up)
    slope = low(phi_up + upper * (0.3989422804014327 * jnp.exp(-0.5 * upper * upper)))
    down_other = plane.swap(low(across(active[:, ff:], cot_all)))
    weight_down = with_mate(gate([weight_down], down_other)[0] if kernels else weight_down, 0)
    kept = []

    def upper_back(token):
        kept.append(low(against(hold(cot_all, token), weight_down) * slope.astype(f32)))
        return kept[0]

    def normed_back(token):
        return low(against(kept[0], weight_up))

    feed = low(dot(active, weight_down))
    if kernels:
        down_other = gate([down_other], feed[:16])[0]
    down_grad = low(across(active[:, :ff], cot_all) + down_other.astype(f32))
    down_mine = lax.psum_scatter(down_grad, "fsdp", scatter_dimension=0, tiled=True)
    feed, (upper_grad, partial) = plane.scatter(feed, (upper_back, normed_back))
    output = low(middle + (feed + bias_down))
    others = []

    def mate_grads(token):
        others.append(plane.swap(low(across(normed_two, hold(upper_grad, token)[:, ff:]))))
        return others[0]

    normed_two_grad, _ = plane.scatter(partial, (mate_grads,))
    gain_back = gate([gain_two[None]], output)[0][0] if kernels else gain_two
    middle_grad = cot_float + norm_input_grad(normed_two_grad, normal_two, inverse_two, gain_back)
    branch_grad = low(middle_grad)
    up_other = gate([others[0]], branch_grad)[0] if kernels else others[0]
    up_grad = low(across(normed_two, upper_grad[:, :ff]) + up_other.astype(f32))
    if kernels:
        up_grad = gate([up_grad], down_mine)[0]
    up_mine = lax.psum_scatter(up_grad, "fsdp", scatter_dimension=0, tiled=True)
    up_bias_grad = jnp.sum(upper_grad.astype(f32), axis=0)
    branch_all, _ = plane.gather(branch_grad)

    shape = (spans // 2, replicas, span_rows, width)
    upstream_far = plane.swap(low(against(branch_all, weight_out[width:])))
    upstream_near = low(against(branch_all, weight_out[:width]))
    upstream = (upstream_near.reshape(shape), upstream_far.reshape(shape))
    fine = kernels and even and hidden % LANES == 0 and block * 2 == LANES and share % (2 * ROW_BLOCK) == 0
    if kernels:
        info = gate([info], up_grad)[0]
        known = (info, projected, (mixed_near, mixed_far), upstream, log_totals, span_rows, heads)
        grads = attend_back_call(*known)
    else:
        allowed = allowed_of(plane, span_rows, own_span, lengths)
        upstream = split(jnp.concatenate(upstream, axis=0))
        query_grad, key_grad, value_grad = attend_back(*parts_of(*projected), upstream, log_totals, allowed)
        query_grad = jnp.pad(to_pieces(query_grad), ((0, 0), (0, 0), (0, MEM_ROWS), (0, 0), (0, 0)))
        grads = jnp.stack([query_grad, to_pieces(key_grad), to_pieces(value_grad)], axis=-2)
        grads = (grads[: spans // 2], grads[spans // 2 :])
    near, far = [g.reshape(count * piece_rows, 3 * width) for g in grads]
    if fine:
        down_found = plane.whole(down_mine)
        near, far = gate([near, far], *[v for name, v in down_found.items() if name != (0, 0)])
    other = plane.swap(far)
    qkv_grad = low(across(normed, near) + across(plane.swap(normed), far))
    if fine:
        qkv_grad = gate([qkv_grad], up_mine)[0]
    qkv_mine = lax.psum_scatter(qkv_grad, "fsdp", scatter_dimension=0, tiled=True)
    both = jnp.concatenate([near, gate([other], qkv_grad)[0] if kernels else other], axis=1)
    partial = low(against(both, jnp.concatenate([weight_qkv, qkv_mate], axis=1)))
    def mate_out(token):
        others.append(low(across(attended[:, width:], hold(branch_all, token))))
        return others[-1]

    def own_out(token):
        return low(across(attended[:, :width], branch_all) + plane.swap(others[-1]).astype(f32))

    if fine:
        own_replica = lax.axis_index("replica")
        names = np.array(plane.near + plane.far, np.int32)
        table = jnp.bitwise_xor(own_replica, names[:, 0]) * spans + jnp.bitwise_xor(own_span, names[:, 1])
        table = table.astype(jnp.int32)
    normed_grad, (_, out_grad_w) = plane.scatter(partial, (mate_out, own_out))
    rows_grad = norm_input_grad(normed_grad, normal_one, inverse_one, gain_one)
    input_grad = middle_grad + rows_grad[:span_rows]
    slots_all = {0: rows_grad[span_rows:]}
    bit = 1
    while bit < spans:
        for value, rows in list(slots_all.items()):
            slots_all[value ^ bit] = plane.swap(rows, ("ctx", bit))
        bit *= 2
    slots_grad = jnp.zeros((spans * MEM_ROWS, D), f32)
    for value, rows in slots_all.items():
        start = jnp.bitwise_xor(own_span, value) * MEM_ROWS
        slots_grad = lax.dynamic_update_slice_in_dim(slots_grad, rows, start, 0)
    slots_grad = slots_grad[:SUMM]

    def spot(values, full, groups, size, device):
        base = jnp.zeros((groups, full // groups), f32)
        return lax.dynamic_update_slice_in_dim(base, values.reshape(groups, size), device * size, 1).reshape(full)

    bias_grads = (jnp.sum(near.astype(f32), axis=0) + jnp.sum(far.astype(f32), axis=0)).reshape(pairs, 3, -1)
    parts = [
        spot(bias_grads[:, 0], D, groups, block, index),
        spot(bias_grads[:, 2], D, groups, block, index),
        jnp.sum(branch_grad.astype(f32), axis=0),
        jnp.sum(normed_two_grad * normal_two, axis=0),
        jnp.sum(normed_two_grad, axis=0),
        jnp.sum(cot_float, axis=0),
        spot(up_bias_grad[:ff], ff * team, owners, hidden, index)
        + spot(up_bias_grad[ff:], ff * team, owners, hidden, mate),
    ]
    sums = jnp.sum(partial.astype(f32), axis=0)
    parts += [(jnp.sum(partial.astype(f32) * normed.astype(f32), axis=0) - shift_one * sums) / gain_one, sums]
    vector = low(jnp.concatenate([part.reshape(owners, -1) for part in parts], axis=1))
    used = vector.shape[1]
    extra = -(-used // (16 * D)) * 16
    vector = jnp.pad(vector, ((0, 0), (0, extra * D - used))).reshape(owners, extra, D)

    def columns_all(full, groups, size):
        full = full.reshape(team, share, groups, size)
        return jnp.moveaxis(full, 0, 2).reshape(share, -1).astype(f32)

    if fine:
        qkv_found = plane.whole(qkv_mine)
        down_all = place_rows(table, plane.complete(down_found, True))
        sides = plane.complete(qkv_found, True, (down_all,))
        devices = jnp.arange(team, dtype=jnp.int32)
        up_full = lax.all_gather(gate([up_mine], qkv_mine)[0], PLANE, axis=0, tiled=False)
        up_all = place_columns(
            functools.partial(place_up_kernel, owners), devices, [[up_full] * team], share, ff * team
        )
        out_rows = gate([out_grad_w], qkv_mine)[0].reshape(owners, block, D)
        joined = jnp.concatenate([out_rows, vector], axis=1).reshape(-1, D)
        out_mine = lax.psum_scatter(joined, "fsdp", scatter_dimension=0, tiled=True)
        qkv_all = place_columns(functools.partial(place_heads_kernel, order), table, sides, share, 3 * D)
        out_mine = gate([out_mine], sides[0][plane.half - 1])[0]
        out_sides = plane.complete(plane.whole(out_mine), False)
        out_all = place_rows(table, out_sides, block)
        vectors = sum(rows[block:].astype(f32) for rows in out_sides[0])
    else:
        down_all = lax.all_gather(down_mine, PLANE, axis=0, tiled=True).astype(f32)
        up_all = columns_all(lax.all_gather(up_mine, PLANE, axis=0, tiled=False), owners, hidden)
        qkv_full = lax.all_gather(qkv_mine, PLANE, axis=0, tiled=False).reshape(team, share, 3 * groups, block)
        qkv_full = jnp.concatenate([qkv_full[:, :, order.index(g)][:, :, None] for g in range(3 * groups)], axis=2)
        qkv_all = columns_all(qkv_full, 3 * groups, block)
        if even:
            out_mine = lax.psum_scatter(out_grad_w, "fsdp", scatter_dimension=0, tiled=True)
            out_all = lax.all_gather(out_mine, PLANE, axis=0, tiled=True).astype(f32)
        else:
            placed = lax.dynamic_update_slice_in_dim(jnp.zeros((D, D), bf16), out_grad_w, index * width, 0)
            out_all = lax.psum(lax.psum_scatter(placed, "fsdp", scatter_dimension=0, tiled=True), PLANE).astype(f32)
        vectors = lax.psum(lax.psum_scatter(vector, "fsdp", scatter_dimension=0, tiled=True), PLANE).astype(f32)
    vectors = vectors.reshape(-1)
    take = lambda i: vectors[i * share : (i + 1) * share]
    up_end = 6 * share + ff * team // owners
    return (
        output.reshape(hidden_in.shape),
        input_grad.reshape(hidden_in.shape),
        slots_grad.reshape(memory_rows.shape),
        vectors[up_end : up_end + share],
        vectors[up_end + share : up_end + 2 * share],
        qkv_all,
        take(0),
        take(1),
        out_all,
        take(2),
        take(3),
        take(4),
        up_all,
        vectors[6 * share : up_end],
        down_all,
        take(5),
    )


def solution(mesh):
    rows = P(("fsdp", "replica"), "ctx", None)
    part = P("fsdp")
    table = P("fsdp", None)
    whole = P(("fsdp", "replica"), None, None)
    return jax.shard_map(
        shards,
        mesh=mesh,
        in_specs=(
            rows,
            whole,
            P(("fsdp", "replica")),
            rows,
            part,
            part,
            table,
            part,
            part,
            table,
            part,
            part,
            part,
            table,
            part,
            table,
            part,
        ),
        out_specs=(
            rows,
            rows,
            whole,
            part,
            part,
            table,
            part,
            part,
            table,
            part,
            part,
            part,
            table,
            part,
            table,
            part,
        ),
        check_vma=False,
    )
```

```python
import functools

import jax
import jax.numpy as jnp
import numpy as np
from jax import lax
from jax.experimental import pallas as pl
from jax.experimental.pallas import tpu as pltpu
from jax.sharding import PartitionSpec as P

D = 2048
HEADS = 32
HEAD_DIM = 64
SUMM = 50
SEQ_LEN = 1088
SEG = 1038
MEM_ROWS = 16
LANES = 128
QUERY_BLOCK = 256
ROW_BLOCK = 64

epsilon = 1e-05
masked = -1e30
f32 = jnp.float32
bf16 = jnp.bfloat16
PLANE = ("replica", "ctx")


def dot(left, right):
    return jnp.dot(left, right, preferred_element_type=f32)


def across(left, right):
    return lax.dot_general(left, right, (((0,), (0,)), ((), ())), preferred_element_type=f32)


def against(left, right):
    return lax.dot_general(left, right, (((1,), (1,)), ((), ())), preferred_element_type=f32)


def normal_of(rows):
    centred = rows - jnp.mean(rows, axis=-1, keepdims=True)
    inverse = lax.rsqrt(jnp.mean(centred * centred, axis=-1, keepdims=True) + epsilon)
    return centred * inverse, inverse


def norm_input_grad(upstream, normal, inverse, weight):
    scaled = upstream * weight
    centre = jnp.mean(scaled, axis=-1, keepdims=True)
    slope = jnp.mean(scaled * normal, axis=-1, keepdims=True)
    return inverse * (scaled - centre - normal * slope)


class Plane:
    def __init__(self):
        self.replicas = lax.axis_size("replica")
        self.spans = lax.axis_size("ctx")
        self.sizes = {"replica": self.replicas, "ctx": self.spans}
        self.slow = []
        for axis, bit in (("replica", 1), ("ctx", 2)):
            while bit < self.sizes[axis]:
                self.slow.append((axis, bit))
                bit *= 2
        self.fast = ("ctx", 1)
        self.near = [(r, v) for v in range(0, self.spans, 2) for r in range(self.replicas)]
        self.far = [(r, v + 1) for r, v in self.near]
        self.half = len(self.near)

    def swap(self, array, stage=None):
        axis, bit = stage or self.fast
        return lax.ppermute(array, axis, [(i, i ^ bit) for i in range(self.sizes[axis])])

    def step(self, name, stage):
        axis, bit = stage
        return (name[0] ^ bit, name[1]) if axis == "replica" else (name[0], name[1] ^ bit)

    def bit(self, name, stage):
        axis, bit = stage
        return (name[0] if axis == "replica" else name[1]) & bit

    def send(self, rows, cut=None):
        cut = cut or cut_of(rows.shape[0])
        sides = [rows[:cut], rows[cut:]]
        return [[self.swap(side, stage) for stage in plan] for side, plan in zip(sides, (self.slow, self.slow[::-1]))]

    def travel(self, rows, fills=(), cut=None, first=None):
        cut = cut or cut_of(rows.shape[0])
        plans = [self.slow, self.slow[::-1]]
        found = [{(0, 0): rows[:cut]}, {(0, 0): rows[cut:]}]
        first = first or self.send(rows, cut)
        results = []
        for level in range(len(self.slow)):
            arrived = []
            for side in range(2):
                stage = plans[side][level]
                for name, value in list(found[side].items()):
                    moved = first[side][level] if name == (0, 0) else self.swap(value, stage)
                    name = self.step(name, stage)
                    found[side][name] = moved
                    if level == 0 or name != self.step((0, 0), stage):
                        arrived.append((side, name))
            if level < len(fills) and fills[level] is not None:
                filled = fills[level]()
                side, name = arrived[-1]
                found[side][name], filled = lax.optimization_barrier((found[side][name], filled))
                results.append(filled)
        return found, results

    def gather(self, rows, fills=(), first=None):
        found, results = self.travel(rows, fills, None, first)
        return jnp.concatenate([found[side][name] for name in self.near for side in range(2)], axis=0), results

    def sides(self, found):
        sides = [[found[side][name] for name in self.near] for side in range(2)]
        return [side + [self.swap(value) for value in side] for side in sides]

    def spread(self, block, cut=None, first=None):
        return self.sides(self.travel(block, (), cut, first)[0])

    def scatter(self, partial, fills=(), before=()):
        count = partial.shape[0] // self.half
        cut = cut_of(count)
        held = [{}, {}]
        for index, name in enumerate(self.near):
            held[0][name] = partial[index * count : index * count + cut]
            held[1][name] = partial[index * count + cut : (index + 1) * count]
        plans = [self.slow, self.slow[::-1]]
        results = []
        for level in range(len(self.slow)):
            moves = []
            for side in range(2):
                stage = plans[side][level]
                for name in reversed(held[side]):
                    if not self.bit(name, stage):
                        moves.append((side, name, held[side][self.step(name, stage)], stage))
            filled = None
            if before and level == 0:
                moves = [(*move[:2], gate([move[2]], *before)[0], move[3]) if move[1] != (0, 0) else move for move in moves]
            if level < len(fills):
                filled = fills[level](moves[0][2])
            kept = [{}, {}]
            for number, (side, name, value, stage) in enumerate(moves):
                moved = self.swap(value, stage)
                if filled is not None and number == len(moves) - 1:
                    moved, filled = lax.optimization_barrier((moved, filled))
                    results.append(filled)
                total = held[side][name].astype(f32) + moved.astype(f32)
                kept[side][name] = total if name == (0, 0) else total.astype(bf16)
            held = kept
        for fill in fills[len(self.slow) :]:
            results.append(fill(held[0][(0, 0)]))
        return jnp.concatenate([held[0][(0, 0)], held[1][(0, 0)]], axis=0), results

    def whole(self, block):
        found = {(0, 0): block}
        firsts = [self.step((0, 0), stage) for stage in self.slow]
        for name, stage in zip(firsts, self.slow):
            found[name] = self.swap(block, stage)
        return found

    def extend(self, found, turned):
        for stage in self.slow[::-1] if turned else self.slow:
            for name, value in list(found.items()):
                name = self.step(name, stage)
                if name not in found:
                    found[name] = self.swap(value, stage)

    def complete(self, found, turned, together=False):
        names = [name for name in found if name != (0, 0)]
        if together:
            found = {(0, 0): found[(0, 0)], **dict(zip(names, gate([found[name] for name in names])))}
        self.extend(found, turned)
        near = [found[name] for name in self.near]
        return [near + [self.swap(value) for value in near]]


def cut_of(count):
    return (count // 2 + 15) // 16 * 16


def columns_of(weight, groups, index, width, order=None):
    span = weight.shape[1] // groups
    order = range(groups) if order is None else order
    return jnp.concatenate(
        [lax.dynamic_slice_in_dim(weight, g * span + index * width, width, 1) for g in order], axis=1
    )


def allowed_of(plane, span_rows, own, lengths):
    places, slots = [], []
    for value in [v for _, v in plane.near + plane.far if _ == 0]:
        base = own ^ value
        rows = jnp.arange(span_rows, dtype=jnp.int32) + base * span_rows
        mem = jnp.arange(MEM_ROWS, dtype=jnp.int32) + base * MEM_ROWS
        places.append((rows, mem))
    far = jnp.int32(1 << 30)
    queries = jnp.concatenate([rows for rows, _ in places])
    keys = jnp.concatenate([jnp.concatenate([rows, jnp.where(mem < SUMM, -1, far)]) for rows, mem in places])
    causal = keys[None, :] <= queries[:, None]
    present = (keys[None, :] < lengths[:, None]) | (keys[None, :] >= SEG)
    return causal[None] & present[:, None, :]


def attend(query, key, value, allowed):
    scores = jnp.einsum("gqhd,gkhd->ghqk", query, key, preferred_element_type=f32)
    scores = jnp.where(allowed[:, None], scores, masked)
    largest = jnp.max(scores, axis=-1, keepdims=True)
    expanded = jnp.exp(scores - largest)
    totals = jnp.sum(expanded, axis=-1, keepdims=True)
    weights = (expanded / totals).astype(bf16)
    mixed = jnp.einsum("ghqk,gkhd->gqhd", weights, value, preferred_element_type=f32)
    return mixed.astype(bf16), largest + jnp.log(totals)


def attend_back(query, key, value, upstream, log_totals, allowed):
    scores = jnp.einsum("gqhd,gkhd->ghqk", query, key, preferred_element_type=f32)
    scores = jnp.where(allowed[:, None], scores, masked)
    weights = jnp.exp(scores - log_totals)
    value_grad = jnp.einsum("ghqk,gqhd->gkhd", weights.astype(bf16), upstream, preferred_element_type=f32)
    weight_grad = jnp.einsum("gqhd,gkhd->ghqk", upstream, value, preferred_element_type=f32)
    centre = jnp.sum(weights * weight_grad, axis=-1, keepdims=True)
    score_grad = (weights * (weight_grad - centre)).astype(bf16)
    query_grad = jnp.einsum("ghqk,gkhd->gqhd", score_grad, key, preferred_element_type=f32)
    key_grad = jnp.einsum("ghqk,gqhd->gkhd", score_grad, query, preferred_element_type=f32)
    return query_grad.astype(bf16) * 0.125, key_grad.astype(bf16), value_grad.astype(bf16)


def blocks_of(count):
    starts = list(range(0, count, QUERY_BLOCK))
    return [(s, min(QUERY_BLOCK, count - s)) for s in starts]


def piece_of(own, c):
    v = jnp.bitwise_xor(own, c)
    return jnp.right_shift(v, 1), jnp.bitwise_and(v, 1) == 0


def to_sequence(spans, span_rows, own, near, far, target, with_slots=True):
    base = spans * MEM_ROWS
    for c in range(spans):
        slot, is_near = piece_of(own, c)
        rows = jnp.where(is_near, near[slot, 0, :span_rows, :], far[slot, 0, :span_rows, :])
        target[base + c * span_rows : base + (c + 1) * span_rows] = rows
        if with_slots:
            rows = jnp.where(is_near, near[slot, 0, span_rows:, :], far[slot, 0, span_rows:, :])
            target[c * MEM_ROWS : (c + 1) * MEM_ROWS] = rows
    if not with_slots:
        target[:base] = jnp.zeros((base, target.shape[1]), target.dtype)


def key_bias(length, spans, seq_len):
    base = spans * MEM_ROWS
    shape = (base + seq_len, LANES)
    row = lax.broadcasted_iota(jnp.int32, shape, 0)
    place = row - base
    good = (row < SUMM) | ((place >= 0) & ((place < length) | (place >= SEG)))
    return jnp.where(good, 0.0, masked).astype(f32)


def head_masks(count):
    lane = lax.broadcasted_iota(jnp.int32, (count, LANES), 1)
    return lane < HEAD_DIM, lane == HEAD_DIM, lane == 0


def headed(array, masks, head):
    return jnp.where(masks[0] if head == 0 else ~masks[0], array, 0.0)


def scores_of(keys, query, start, size, base):
    stop = start + size
    scores = against(keys[:stop], query[start:stop])
    tail = scores[start:stop]
    row = lax.broadcasted_iota(jnp.int32, (size, size), 0)
    column = lax.broadcasted_iota(jnp.int32, (size, size), 1)
    seen = row <= column
    if start < base:
        seen = seen | (row < base - start)
    tail = jnp.where(seen, tail, masked)
    return tail if start == 0 else jnp.concatenate([scores[:start], tail], axis=0)


def attend_kernel(spans, span_rows, info, qn, qf, kn, kf, vn, vf, on, of, lse_ref, q_all, k_all, v_all, o_all):
    count = k_all.shape[0]
    base = spans * MEM_ROWS
    own = info[0]
    to_sequence(spans, span_rows, own, qn, qf, q_all)
    to_sequence(spans, span_rows, own, kn, kf, k_all)
    to_sequence(spans, span_rows, own, vn, vf, v_all)
    masks = head_masks(count)
    bias = key_bias(info[1 + pl.program_id(0)], spans, count - base)
    query, key = q_all[...].astype(f32), k_all[...].astype(f32)
    values = v_all[...].astype(f32).T.astype(bf16)
    queries, keys = [], []
    for head in range(2):
        flag = masks[1] if head == 0 else masks[2]
        queries.append((headed(query, masks, head) + jnp.where(flag, 1.0, 0.0)).astype(bf16))
        keys.append((headed(key, masks, head) + jnp.where(flag, bias, 0.0)).astype(bf16))
    for start, size in blocks_of(count):
        tops = []
        for head in range(2):
            scores = scores_of(keys[head], queries[head], start, size, base)
            largest = jnp.max(scores, axis=0, keepdims=True)
            expanded = jnp.exp(scores - largest)
            totals = jnp.sum(expanded, axis=0, keepdims=True)
            lse_ref[0, 0, head : head + 1, start : start + size] = largest + jnp.log(totals)
            mixed = jnp.dot(values[:, : start + size], expanded.astype(bf16), preferred_element_type=f32)
            tops.append(mixed[head * HEAD_DIM : (head + 1) * HEAD_DIM] / totals)
        o_all[start : start + size] = jnp.concatenate(tops, axis=0).T.astype(bf16)
    for c in range(spans):
        slot, is_near = piece_of(own, c)
        for target, chosen in ((on, is_near), (of, jnp.logical_not(is_near))):

            @pl.when(chosen)
            def _(c=c, slot=slot, target=target):
                target[slot, 0] = o_all[base + c * span_rows : base + (c + 1) * span_rows]


def attend_back_kernel(spans, span_rows, info, qn, qf, kn, kf, vn, vf, on, of, gn, gf, lse_ref, *rest):
    d_near, d_far, q_all, k_all, v_all, o_all, g_all, dq, dk, dv = rest[-10:]
    count = k_all.shape[0]
    base = spans * MEM_ROWS
    own = info[0]
    to_sequence(spans, span_rows, own, qn, qf, q_all)
    to_sequence(spans, span_rows, own, kn, kf, k_all)
    to_sequence(spans, span_rows, own, vn, vf, v_all)
    to_sequence(spans, span_rows, own, on, of, o_all, False)
    to_sequence(spans, span_rows, own, gn, gf, g_all, False)
    masks = head_masks(count)
    bias = key_bias(info[1 + pl.program_id(0)], spans, count - base)
    query, key, grad = q_all[...].astype(f32), k_all[...].astype(f32), g_all[...].astype(f32)
    overlap = (grad * o_all[...].astype(f32)).T
    keys_t = key.T.astype(bf16)
    values = v_all[...]
    plain_q, plain_g, flag_q, flag_k, deltas = [], [], [], [], []
    for head in range(2):
        flag = masks[1] if head == 0 else masks[2]
        own_q = headed(query, masks, head)
        plain_q.append(own_q.astype(bf16))
        plain_g.append(headed(grad, masks, head).astype(bf16))
        flag_q.append((own_q + jnp.where(flag, 1.0, 0.0)).astype(bf16))
        flag_k.append((headed(key, masks, head) + jnp.where(flag, bias, 0.0)).astype(bf16))
        deltas.append(jnp.sum(overlap[head * HEAD_DIM : (head + 1) * HEAD_DIM], axis=0, keepdims=True))
    for start, size in reversed(blocks_of(count)):
        stop = start + size
        tops, weights_low, slopes = [], [], []
        for head in range(2):
            scores = scores_of(flag_k[head], flag_q[head], start, size, base)
            weights = jnp.exp(scores - lse_ref[0, 0, head : head + 1, start:stop])
            weight_grad = against(values[:stop], plain_g[head][start:stop])
            slope = (weights * (weight_grad - deltas[head][:, start:stop])).astype(bf16)
            weights_low.append(weights.astype(bf16))
            slopes.append(slope)
            turned = jnp.dot(keys_t[:, :stop], slope, preferred_element_type=f32)
            tops.append(turned[head * HEAD_DIM : (head + 1) * HEAD_DIM])
        dq[start:stop] = (jnp.concatenate(tops, axis=0).T.astype(bf16).astype(f32) * 0.125).astype(bf16)
        grads = jnp.concatenate([plain_g[0][start:stop], plain_g[1][start:stop]], axis=0)
        queries = jnp.concatenate([plain_q[0][start:stop], plain_q[1][start:stop]], axis=0)
        value_part = jnp.dot(jnp.concatenate(weights_low, axis=1), grads, preferred_element_type=f32)
        key_part = jnp.dot(jnp.concatenate(slopes, axis=1), queries, preferred_element_type=f32)
        if stop == count:
            dv[...] = value_part
            dk[...] = key_part
        else:
            dv[:stop] += value_part
            dk[:stop] += key_part
    for c in range(spans):
        slot, is_near = piece_of(own, c)
        rows = slice(base + c * span_rows, base + (c + 1) * span_rows)
        slots = slice(c * MEM_ROWS, (c + 1) * MEM_ROWS)
        for target, chosen in ((d_near, is_near), (d_far, jnp.logical_not(is_near))):

            @pl.when(chosen)
            def _(slot=slot, rows=rows, slots=slots, target=target):
                for part, source in enumerate((dq, dk, dv)):
                    lanes = slice(part * LANES, (part + 1) * LANES)
                    target[slot, 0, :span_rows, lanes] = source[rows].astype(bf16)
                    low = jnp.zeros((MEM_ROWS, LANES), bf16) if part == 0 else source[slots].astype(bf16)
                    target[slot, 0, span_rows:, lanes] = low


def attend_call(info, near, far, span_rows, heads):
    slots, replicas, rows, _ = near.shape
    spans, pairs = 2 * slots, heads // 2
    count = spans * rows
    piece = lambda part: [pl.BlockSpec((slots, 1, rows, LANES), lambda r, p, info: (0, r, 0, 3 * p + part))] * 2
    mixed = pl.BlockSpec((slots, 1, span_rows, LANES), lambda r, p, info: (0, r, 0, p))
    shape = jax.ShapeDtypeStruct((slots, replicas, span_rows, pairs * LANES), bf16)
    return pl.pallas_call(
        functools.partial(attend_kernel, spans, span_rows),
        out_shape=(shape, shape, jax.ShapeDtypeStruct((replicas, pairs, 2, count), f32)),
        grid_spec=pltpu.PrefetchScalarGridSpec(
            num_scalar_prefetch=1,
            grid=(replicas, pairs),
            in_specs=piece(0) + piece(1) + piece(2),
            out_specs=(mixed, mixed, pl.BlockSpec((1, 1, 2, count), lambda r, p, info: (r, p, 0, 0))),
            scratch_shapes=[pltpu.VMEM((count, LANES), bf16)] * 4,
        ),
        compiler_params=pltpu.CompilerParams(vmem_limit_bytes=56 << 20),
        cost_estimate=pl.CostEstimate(flops=24 * 10**9, bytes_accessed=8 * 10**6, transcendentals=10**7),
        name="attend",
    )(info, near, far, near, far, near, far)


def attend_back_call(info, projected, attended, upstream, log_totals, span_rows, heads):
    slots, replicas, rows, _ = projected[0].shape
    spans, pairs = 2 * slots, heads // 2
    count = spans * rows
    piece = lambda part: [pl.BlockSpec((slots, 1, rows, LANES), lambda r, p, info: (0, r, 0, 3 * p + part))] * 2
    plain = [pl.BlockSpec((slots, 1, span_rows, LANES), lambda r, p, info: (0, r, 0, p))] * 4
    specs = piece(0) + piece(1) + piece(2) + plain
    specs.append(pl.BlockSpec((1, 1, 2, count), lambda r, p, info: (r, p, 0, 0)))
    inputs = [*projected, *projected, *projected, *attended, *upstream, log_totals]
    shape = jax.ShapeDtypeStruct((slots, replicas, rows, 3 * pairs * LANES), bf16)
    return pl.pallas_call(
        functools.partial(attend_back_kernel, spans, span_rows),
        out_shape=(shape, shape),
        grid_spec=pltpu.PrefetchScalarGridSpec(
            num_scalar_prefetch=1,
            grid=(replicas, pairs),
            in_specs=specs,
            out_specs=[pl.BlockSpec((slots, 1, rows, 3 * LANES), lambda r, p, info: (0, r, 0, p))] * 2,
            scratch_shapes=[pltpu.VMEM((count, LANES), bf16)] * 6 + [pltpu.VMEM((count, LANES), f32)] * 2,
        ),
        compiler_params=pltpu.CompilerParams(vmem_limit_bytes=56 << 20),
        cost_estimate=pl.CostEstimate(flops=30 * 10**9, bytes_accessed=16 * 10**6, transcendentals=10**7),
        name="attend_back",
    )(info, *inputs)


def place_up_kernel(owners, table, *refs):
    target = refs[-1]
    width = refs[0].shape[1] // owners
    team = target.shape[1] // (owners * width)
    for k in range(team):
        for z in range(owners):
            lanes = pl.ds(pl.multiple_of((z * team + table[k]) * width, width), width)
            target[:, lanes] = refs[k][:, z * width : (z + 1) * width].astype(f32)


def place_heads_kernel(order, table, *refs):
    target = refs[-1]
    groups = len(order)
    width = refs[0].shape[1] // groups
    team = target.shape[1] // (groups * width)
    half = team // 2
    odd = table[0] % 2 == 1
    for k in range(half):
        mine, other = refs[k][...].astype(f32), refs[k + half][...].astype(f32)
        first = jnp.where(odd, other, mine)
        second = jnp.where(odd, mine, other)
        place = table[k] // 2
        for position, g in enumerate(order):
            cut = slice(position * width, (position + 1) * width)
            lanes = pl.ds(pl.multiple_of((g * half + place) * 2 * width, 2 * width), 2 * width)
            target[:, lanes] = jnp.concatenate([first[:, cut], second[:, cut]], axis=1)


def place_columns(kernel, table, sides, rows, columns):
    result = None
    size = rows // len(sides)
    for number, side in enumerate(sides):
        inputs = list(side)
        if side[0].ndim == 3:
            block = (None, ROW_BLOCK, side[0].shape[2])
            specs = [pl.BlockSpec(block, lambda i, t, k=k: (k, i, 0)) for k in range(len(side))]
        else:
            specs = [pl.BlockSpec((ROW_BLOCK, side[0].shape[1]), lambda i, t: (i, 0))] * len(side)
        shift = number * size // ROW_BLOCK
        result = placed(kernel, table, inputs, specs, result, (rows, columns), (ROW_BLOCK, columns), size // ROW_BLOCK, lambda i, t: (i + shift, 0))
    return result


def placed(kernel, table, inputs, specs, result, shape, block, steps, index):
    aliases = {}
    if result is not None:
        inputs.append(result)
        specs.append(pl.BlockSpec(memory_space=pl.ANY))
        aliases = {len(inputs): 0}
    return pl.pallas_call(
        kernel,
        out_shape=jax.ShapeDtypeStruct(shape, f32),
        grid_spec=pltpu.PrefetchScalarGridSpec(
            num_scalar_prefetch=1,
            grid=(steps,),
            in_specs=specs,
            out_specs=pl.BlockSpec(block, index),
        ),
        input_output_aliases=aliases,
        compiler_params=pltpu.CompilerParams(vmem_limit_bytes=40 << 20),
        cost_estimate=pl.CostEstimate(flops=0, bytes_accessed=6 * steps * block[0] * block[1], transcendentals=0),
        name="place",
    )(table, *inputs)


def place_rows_kernel(team, table, *refs):
    target = refs[-1]
    for k in range(team):

        @pl.when(pl.program_id(0) == k)
        def _(k=k):
            target[...] = refs[k][...].astype(f32)


def place_rows(table, sides, used=None):
    team = len(sides[0])
    result = None
    count = len(sides)
    for number, side in enumerate(sides):
        size, columns = (used or side[0].shape[0]), side[0].shape[1]
        specs = [pl.BlockSpec((size, columns), lambda i, t: (0, 0), pipeline_mode=pl.Buffered(1))] * team
        kernel = functools.partial(place_rows_kernel, team)
        shape = (count * size * team, columns)
        result = placed(kernel, table, list(side), specs, result, shape, (size, columns), team, lambda i, t, number=number: (count * t[i] + number, 0))
    return result


def hold(value, *others):
    return lax.optimization_barrier((value, *others))[0]


def gate(values, *others):
    values = list(values)
    anywhere = pl.BlockSpec(memory_space=pl.ANY)
    return pl.pallas_call(
        lambda *refs: None,
        out_shape=[jax.ShapeDtypeStruct(v.shape, v.dtype) for v in values],
        in_specs=[anywhere] * (len(values) + len(others)),
        out_specs=[anywhere] * len(values),
        input_output_aliases={i: i for i in range(len(values))},
        name="gate",
    )(*values, *others)


def shards(
    hidden_in,
    memory_rows,
    seg_len,
    out_grad,
    first_gain,
    first_shift,
    qkv_weight,
    query_bias,
    value_bias,
    out_weight,
    out_bias,
    second_gain,
    second_shift,
    up_weight,
    up_bias,
    down_weight,
    down_bias,
):
    plane = Plane()
    owners = lax.axis_size("fsdp")
    replicas, spans = plane.replicas, plane.spans
    team = replicas * spans
    count = plane.half
    owner = lax.axis_index("fsdp")
    own_span = lax.axis_index("ctx")
    index = lax.axis_index("replica") * spans + own_span
    mate = jnp.bitwise_xor(index, 1)
    share = D // owners
    span_rows = hidden_in.shape[1]
    piece_rows = span_rows + MEM_ROWS
    heads = HEADS // team
    width = heads * HEAD_DIM
    hidden = up_bias.shape[0] // team
    ff = hidden * owners
    low = lambda array: array.astype(bf16)

    even = heads % owners == 0
    block = width // owners if even else width
    groups = owners if even else 1
    pairs = max(heads // 2, 1)
    inner = groups // pairs if groups > 1 else 1
    order = [part * groups + pair * inner + i for pair in range(pairs) for part in range(3) for i in range(inner)]
    columns_qkv = columns_of(qkv_weight, 3 * groups, index, block, order)
    weight_qkv = lax.all_gather(columns_qkv, "fsdp", axis=0, tiled=True)
    small = jnp.concatenate(
        [first_gain, first_shift, query_bias, value_bias, out_bias, second_gain, second_shift, down_bias, up_bias]
    )
    small = lax.all_gather(hold(small, columns_qkv).reshape(-1, 128), "fsdp", axis=0, tiled=True)
    small = small.reshape(owners, -1).astype(f32)
    vectors = [small[:, i * share : (i + 1) * share].reshape(D) for i in range(8)]
    gain_one, shift_one, bias_query, bias_value, bias_out, gain_two, shift_two, bias_down = vectors
    bias_up = jnp.concatenate(
        [lax.dynamic_slice_in_dim(small[:, 8 * share :], i * hidden, hidden, 1).reshape(ff) for i in (index, mate)]
    )
    if even:
        rows_out = lax.dynamic_slice_in_dim(out_weight, index * block, block, 0)
        weight_out = lax.all_gather(rows_out, "fsdp", axis=0, tiled=True)
    else:
        weight_out = lax.dynamic_slice_in_dim(
            lax.all_gather(out_weight, "fsdp", axis=0, tiled=True), index * width, width, 0
        )
    weight_up = lax.all_gather(columns_of(up_weight, owners, index, hidden), "fsdp", axis=0, tiled=True)
    weight_down = lax.all_gather(
        lax.dynamic_slice_in_dim(down_weight, index * hidden, hidden, 0), "fsdp", axis=0, tiled=True
    )
    with_mate = lambda weight, axis: jnp.concatenate([weight, plane.swap(weight)], axis=axis)

    cotangent = out_grad.reshape(span_rows, D)
    cot_float = cotangent.astype(f32)
    cot_first = plane.send(cotangent)

    tokens = hold(hidden_in, cot_first).reshape(span_rows, D)
    slots = jnp.pad(memory_rows.reshape(SUMM, D), ((0, spans * MEM_ROWS - SUMM), (0, 0)))
    slots = lax.dynamic_slice_in_dim(slots, own_span * MEM_ROWS, MEM_ROWS, 0)
    own_rows = jnp.concatenate([tokens, slots], axis=0).astype(f32)
    normal_one, inverse_one = normal_of(own_rows)
    lengths = [seg_len]
    for axis, bit in plane.slow:
        if axis == "replica":
            lengths = lengths + [plane.swap(v, (axis, bit)) for v in lengths]
    lengths = jnp.concatenate(lengths)

    normed, _ = plane.gather(hold(low(normal_one * gain_one + shift_one), lengths))
    weight_qkv = hold(weight_qkv, normed)
    qkv_mate = plane.swap(weight_qkv)
    bias_qkv = jnp.concatenate([bias_query, jnp.zeros((D,), f32), bias_value])[None]
    scale_qkv = jnp.asarray(np.repeat([0.125 if g < groups else 1.0 for g in order], block), f32)

    def project(rows, weight, device):
        bias = columns_of(bias_qkv, 3 * groups, device, block, order)[0]
        return low((dot(rows, weight) + bias) * scale_qkv).reshape(spans // 2, replicas, piece_rows, 3 * width)

    kernels = span_rows % 16 == 0 and heads % 2 == 0 and spans % 2 == 0 and SUMM <= spans * MEM_ROWS
    info = jnp.concatenate([own_span[None].astype(jnp.int32), lengths])
    split = lambda a: jnp.moveaxis(a, 1, 0).reshape(replicas, -1, heads, HEAD_DIM)
    to_pieces = lambda a: jnp.moveaxis(a.reshape(replicas, spans, -1, pairs, width // pairs), 0, 1)

    def parts_of(near, far):
        apart = jnp.concatenate([near, far], axis=0).reshape(spans, replicas, piece_rows, pairs, 3, width // pairs)
        return split(apart[:, :, :span_rows, :, 0]), split(apart[..., 1, :]), split(apart[..., 2, :])

    def attend_all():
        near, far = projected
        if kernels:
            return attend_call(info, near, far, span_rows, heads)
        allowed = allowed_of(plane, span_rows, own_span, lengths)
        mixed, totals = attend(*parts_of(near, far), allowed)
        mixed = to_pieces(mixed).reshape(spans, replicas, span_rows, width)
        return mixed[: spans // 2], mixed[spans // 2 :], totals

    projected = [project(normed, weight_qkv, index)]
    projected.append(plane.swap(project(normed, hold(qkv_mate, projected[0]), mate)))
    cot_all, filled = plane.gather(cotangent, (None, attend_all), cot_first)
    mixed_near, mixed_far, log_totals = filled[0]
    attended = jnp.concatenate([mixed_near, plane.swap(mixed_far)], axis=-1).reshape(count * span_rows, 2 * width)
    weight_out = with_mate(hold(weight_out, projected[0]), 0)
    branch, _ = plane.scatter(low(dot(attended, weight_out)))
    bias_out = gate([bias_out[None]], cot_all)[0][0] if kernels else bias_out
    weight_up = with_mate(gate([weight_up], branch)[0] if kernels else weight_up, 1)
    middle = tokens.astype(f32) + (branch + bias_out)
    normal_two, inverse_two = normal_of(middle)
    normed_two, _ = plane.gather(low(normal_two * gain_two + shift_two))

    upper = dot(normed_two, weight_up) + bias_up
    phi_up = 0.5 * (1.0 + lax.erf(upper * 0.7071067811865476))
    active = low(upper * phi_up)
    slope = low(phi_up + upper * (0.3989422804014327 * jnp.exp(-0.5 * upper * upper)))
    down_other = plane.swap(low(across(active[:, ff:], cot_all)))
    weight_down = with_mate(gate([weight_down], down_other)[0] if kernels else weight_down, 0)
    kept = []

    def upper_back(token):
        kept.append(low(against(cot_all, weight_down) * slope.astype(f32)))
        return kept[0]

    def normed_back(token):
        return low(against(kept[0], weight_up))

    feed = low(dot(active, weight_down))
    down_grad = low(across(active[:, :ff], cot_all) + down_other.astype(f32))
    down_mine = lax.psum_scatter(down_grad, "fsdp", scatter_dimension=0, tiled=True)
    feed, (upper_grad, partial) = plane.scatter(feed, (upper_back, normed_back))
    output = low(middle + (feed + bias_down))
    others = []

    later = [upper_grad]

    def mate_grads(token):
        if kernels:
            later[0] = gate([upper_grad], token)[0]
        others.append(plane.swap(low(across(normed_two, later[0][:, ff:]))))
        return others[0]

    normed_two_grad, _ = plane.scatter(partial, (mate_grads,), (feed,) if kernels else ())
    up_other = gate([others[0]], down_mine)[0] if kernels else others[0]
    up_grad = low(across(normed_two, later[0][:, :ff]) + up_other.astype(f32))
    upper_grad = later[0]
    gain_back = gate([gain_two[None]], up_grad[:16])[0][0] if kernels else gain_two
    middle_grad = cot_float + norm_input_grad(normed_two_grad, normal_two, inverse_two, gain_back)
    branch_grad = low(middle_grad)
    up_mine = lax.psum_scatter(up_grad, "fsdp", scatter_dimension=0, tiled=True)
    up_bias_grad = jnp.sum(upper_grad.astype(f32), axis=0)
    branch_all, _ = plane.gather(branch_grad)

    shape = (spans // 2, replicas, span_rows, width)
    upstream_far = plane.swap(low(against(branch_all, weight_out[width:])))
    upstream_near = low(against(branch_all, weight_out[:width]))
    upstream = (upstream_near.reshape(shape), upstream_far.reshape(shape))
    fine = kernels and even and hidden % LANES == 0 and block * 2 == LANES and share % (2 * ROW_BLOCK) == 0
    if kernels:
        known = (info, projected, (mixed_near, mixed_far), upstream, log_totals, span_rows, heads)
        grads = attend_back_call(*known)
    else:
        allowed = allowed_of(plane, span_rows, own_span, lengths)
        upstream = split(jnp.concatenate(upstream, axis=0))
        query_grad, key_grad, value_grad = attend_back(*parts_of(*projected), upstream, log_totals, allowed)
        query_grad = jnp.pad(to_pieces(query_grad), ((0, 0), (0, 0), (0, MEM_ROWS), (0, 0), (0, 0)))
        grads = jnp.stack([query_grad, to_pieces(key_grad), to_pieces(value_grad)], axis=-2)
        grads = (grads[: spans // 2], grads[spans // 2 :])
    near, far = [g.reshape(count * piece_rows, 3 * width) for g in grads]
    if fine:
        down_found = plane.whole(gate([down_mine], upstream_near)[0])
        near, far = gate([near, far], *[v for name, v in down_found.items() if name != (0, 0)])
    other = plane.swap(far)
    qkv_grad = low(across(normed, near) + across(plane.swap(normed), far))
    if fine:
        qkv_grad = gate([qkv_grad], up_mine)[0]
    qkv_mine = lax.psum_scatter(qkv_grad, "fsdp", scatter_dimension=0, tiled=True)
    if fine:
        plane.extend(down_found, True)
        other = gate([other], qkv_grad, down_found[plane.near[-1]])[0]
    elif kernels:
        other = gate([other], qkv_grad)[0]
    both = jnp.concatenate([near, other], axis=1)
    partial = low(against(both, jnp.concatenate([weight_qkv, qkv_mate], axis=1)))
    def mate_out(token):
        others.append(low(across(attended[:, width:], hold(branch_all, token))))
        return others[-1]

    def own_out(token):
        return low(across(attended[:, :width], branch_all) + plane.swap(others[-1]).astype(f32))

    if fine:
        own_replica = lax.axis_index("replica")
        names = np.array(plane.near + plane.far, np.int32)
        table = jnp.bitwise_xor(own_replica, names[:, 0]) * spans + jnp.bitwise_xor(own_span, names[:, 1])
        table = table.astype(jnp.int32)
    normed_grad, (_, out_grad_w) = plane.scatter(partial, (mate_out, own_out))
    rows_grad = norm_input_grad(normed_grad, normal_one, inverse_one, gain_one)
    input_grad = middle_grad + rows_grad[:span_rows]
    slots_all = {0: rows_grad[span_rows:]}
    bit = 1
    while bit < spans:
        for value, rows in list(slots_all.items()):
            slots_all[value ^ bit] = plane.swap(rows, ("ctx", bit))
        bit *= 2
    slots_grad = jnp.zeros((spans * MEM_ROWS, D), f32)
    for value, rows in slots_all.items():
        start = jnp.bitwise_xor(own_span, value) * MEM_ROWS
        slots_grad = lax.dynamic_update_slice_in_dim(slots_grad, rows, start, 0)
    slots_grad = slots_grad[:SUMM]

    def spot(values, full, groups, size, device):
        base = jnp.zeros((groups, full // groups), f32)
        return lax.dynamic_update_slice_in_dim(base, values.reshape(groups, size), device * size, 1).reshape(full)

    bias_grads = (jnp.sum(near.astype(f32), axis=0) + jnp.sum(far.astype(f32), axis=0)).reshape(pairs, 3, -1)
    parts = [
        spot(bias_grads[:, 0], D, groups, block, index),
        spot(bias_grads[:, 2], D, groups, block, index),
        jnp.sum(branch_grad.astype(f32), axis=0),
        jnp.sum(normed_two_grad * normal_two, axis=0),
        jnp.sum(normed_two_grad, axis=0),
        jnp.sum(cot_float, axis=0),
        spot(up_bias_grad[:ff], ff * team, owners, hidden, index)
        + spot(up_bias_grad[ff:], ff * team, owners, hidden, mate),
    ]
    sums = jnp.sum(partial.astype(f32), axis=0)
    parts += [(jnp.sum(partial.astype(f32) * normed.astype(f32), axis=0) - shift_one * sums) / gain_one, sums]
    vector = low(jnp.concatenate([part.reshape(owners, -1) for part in parts], axis=1))
    used = vector.shape[1]
    extra = -(-used // (16 * D)) * 16
    vector = jnp.pad(vector, ((0, 0), (0, extra * D - used))).reshape(owners, extra, D)

    def columns_all(full, groups, size):
        full = full.reshape(team, share, groups, size)
        return jnp.moveaxis(full, 0, 2).reshape(share, -1).astype(f32)

    if fine:
        qkv_found = plane.whole(qkv_mine)
        down_all = place_rows(table, plane.complete(down_found, True))
        sides = plane.complete(qkv_found, True, True)
        devices = jnp.arange(team, dtype=jnp.int32)
        up_full = lax.all_gather(gate([up_mine], qkv_mine)[0], PLANE, axis=0, tiled=False)
        up_all = place_columns(
            functools.partial(place_up_kernel, owners), devices, [[up_full] * team], share, ff * team
        )
        out_rows = gate([out_grad_w], qkv_mine)[0].reshape(owners, block, D)
        joined = jnp.concatenate([out_rows, vector], axis=1).reshape(-1, D)
        out_mine = lax.psum_scatter(joined, "fsdp", scatter_dimension=0, tiled=True)
        qkv_all = place_columns(functools.partial(place_heads_kernel, order), table, sides, share, 3 * D)
        out_mine = gate([out_mine], down_all, *[v for name, v in qkv_found.items() if name != (0, 0)])[0]
        out_sides = plane.complete(plane.whole(out_mine), False)
        out_all = place_rows(table, out_sides, block)
        vectors = sum(rows[block:].astype(f32) for rows in out_sides[0])
    else:
        down_all = lax.all_gather(down_mine, PLANE, axis=0, tiled=True).astype(f32)
        up_all = columns_all(lax.all_gather(up_mine, PLANE, axis=0, tiled=False), owners, hidden)
        qkv_full = lax.all_gather(qkv_mine, PLANE, axis=0, tiled=False).reshape(team, share, 3 * groups, block)
        qkv_full = jnp.concatenate([qkv_full[:, :, order.index(g)][:, :, None] for g in range(3 * groups)], axis=2)
        qkv_all = columns_all(qkv_full, 3 * groups, block)
        if even:
            out_mine = lax.psum_scatter(out_grad_w, "fsdp", scatter_dimension=0, tiled=True)
            out_all = lax.all_gather(out_mine, PLANE, axis=0, tiled=True).astype(f32)
        else:
            placed = lax.dynamic_update_slice_in_dim(jnp.zeros((D, D), bf16), out_grad_w, index * width, 0)
            out_all = lax.psum(lax.psum_scatter(placed, "fsdp", scatter_dimension=0, tiled=True), PLANE).astype(f32)
        vectors = lax.psum(lax.psum_scatter(vector, "fsdp", scatter_dimension=0, tiled=True), PLANE).astype(f32)
    vectors = vectors.reshape(-1)
    take = lambda i: vectors[i * share : (i + 1) * share]
    up_end = 6 * share + ff * team // owners
    return (
        output.reshape(hidden_in.shape),
        input_grad.reshape(hidden_in.shape),
        slots_grad.reshape(memory_rows.shape),
        vectors[up_end : up_end + share],
        vectors[up_end + share : up_end + 2 * share],
        qkv_all,
        take(0),
        take(1),
        out_all,
        take(2),
        take(3),
        take(4),
        up_all,
        vectors[6 * share : up_end],
        down_all,
        take(5),
    )


def solution(mesh):
    rows = P(("fsdp", "replica"), "ctx", None)
    part = P("fsdp")
    table = P("fsdp", None)
    whole = P(("fsdp", "replica"), None, None)
    return jax.shard_map(
        shards,
        mesh=mesh,
        in_specs=(
            rows,
            whole,
            P(("fsdp", "replica")),
            rows,
            part,
            part,
            table,
            part,
            part,
            table,
            part,
            part,
            part,
            table,
            part,
            table,
            part,
        ),
        out_specs=(
            rows,
            rows,
            whole,
            part,
            part,
            table,
            part,
            part,
            table,
            part,
            part,
            part,
            table,
            part,
            table,
            part,
        ),
        check_vma=False,
    )
```

```python
import functools

import jax
import jax.numpy as jnp
import numpy as np
from jax import lax
from jax.experimental import pallas as pl
from jax.experimental.pallas import tpu as pltpu
from jax.sharding import PartitionSpec as P

D = 2048
HEADS = 32
HEAD_DIM = 64
SUMM = 50
SEQ_LEN = 1088
SEG = 1038
MEM_ROWS = 16
LANES = 128
QUERY_BLOCK = 256
ROW_BLOCK = 64

epsilon = 1e-05
masked = -1e30
f32 = jnp.float32
bf16 = jnp.bfloat16
PLANE = ("replica", "ctx")


def dot(left, right):
    return jnp.dot(left, right, preferred_element_type=f32)


def across(left, right):
    return lax.dot_general(left, right, (((0,), (0,)), ((), ())), preferred_element_type=f32)


def against(left, right):
    return lax.dot_general(left, right, (((1,), (1,)), ((), ())), preferred_element_type=f32)


def normal_of(rows):
    centred = rows - jnp.mean(rows, axis=-1, keepdims=True)
    inverse = lax.rsqrt(jnp.mean(centred * centred, axis=-1, keepdims=True) + epsilon)
    return centred * inverse, inverse


def norm_input_grad(upstream, normal, inverse, weight):
    scaled = upstream * weight
    centre = jnp.mean(scaled, axis=-1, keepdims=True)
    slope = jnp.mean(scaled * normal, axis=-1, keepdims=True)
    return inverse * (scaled - centre - normal * slope)


class Plane:
    def __init__(self):
        self.replicas = lax.axis_size("replica")
        self.spans = lax.axis_size("ctx")
        self.sizes = {"replica": self.replicas, "ctx": self.spans}
        self.slow = []
        for axis, bit in (("replica", 1), ("ctx", 2)):
            while bit < self.sizes[axis]:
                self.slow.append((axis, bit))
                bit *= 2
        self.fast = ("ctx", 1)
        self.near = [(r, v) for v in range(0, self.spans, 2) for r in range(self.replicas)]
        self.far = [(r, v + 1) for r, v in self.near]
        self.half = len(self.near)

    def swap(self, array, stage=None):
        axis, bit = stage or self.fast
        return lax.ppermute(array, axis, [(i, i ^ bit) for i in range(self.sizes[axis])])

    def step(self, name, stage):
        axis, bit = stage
        return (name[0] ^ bit, name[1]) if axis == "replica" else (name[0], name[1] ^ bit)

    def bit(self, name, stage):
        axis, bit = stage
        return (name[0] if axis == "replica" else name[1]) & bit

    def send(self, rows, cut=None):
        cut = cut or cut_of(rows.shape[0])
        sides = [rows[:cut], rows[cut:]]
        return [[self.swap(side, stage) for stage in plan] for side, plan in zip(sides, (self.slow, self.slow[::-1]))]

    def travel(self, rows, fills=(), cut=None, first=None):
        cut = cut or cut_of(rows.shape[0])
        plans = [self.slow, self.slow[::-1]]
        found = [{(0, 0): rows[:cut]}, {(0, 0): rows[cut:]}]
        first = first or self.send(rows, cut)
        results = []
        for level in range(len(self.slow)):
            arrived = []
            for side in range(2):
                stage = plans[side][level]
                for name, value in list(found[side].items()):
                    moved = first[side][level] if name == (0, 0) else self.swap(value, stage)
                    name = self.step(name, stage)
                    found[side][name] = moved
                    if level == 0 or name != self.step((0, 0), stage):
                        arrived.append((side, name))
            if level < len(fills) and fills[level] is not None:
                filled = fills[level]()
                side, name = arrived[-1]
                found[side][name], filled = lax.optimization_barrier((found[side][name], filled))
                results.append(filled)
        return found, results

    def gather(self, rows, fills=(), first=None):
        found, results = self.travel(rows, fills, None, first)
        return jnp.concatenate([found[side][name] for name in self.near for side in range(2)], axis=0), results

    def sides(self, found):
        sides = [[found[side][name] for name in self.near] for side in range(2)]
        return [side + [self.swap(value) for value in side] for side in sides]

    def spread(self, block, cut=None, first=None):
        return self.sides(self.travel(block, (), cut, first)[0])

    def scatter(self, partial, fills=(), before=()):
        count = partial.shape[0] // self.half
        cut = cut_of(count)
        held = [{}, {}]
        for index, name in enumerate(self.near):
            held[0][name] = partial[index * count : index * count + cut]
            held[1][name] = partial[index * count + cut : (index + 1) * count]
        plans = [self.slow, self.slow[::-1]]
        results = []
        for level in range(len(self.slow)):
            moves = []
            for side in range(2):
                stage = plans[side][level]
                for name in reversed(held[side]):
                    if not self.bit(name, stage):
                        moves.append((side, name, held[side][self.step(name, stage)], stage))
            filled = None
            if before and level == 0:
                moves = [(*move[:2], gate([move[2]], *before)[0], move[3]) if move[1] != (0, 0) else move for move in moves]
            if level < len(fills) and fills[level] is not None:
                filled = fills[level](moves[0][2])
            kept = [{}, {}]
            for number, (side, name, value, stage) in enumerate(moves):
                moved = self.swap(value, stage)
                if filled is not None and number == len(moves) - 1:
                    moved, filled = lax.optimization_barrier((moved, filled))
                    results.append(filled)
                total = held[side][name].astype(f32) + moved.astype(f32)
                kept[side][name] = total if name == (0, 0) else total.astype(bf16)
            held = kept
        for fill in fills[len(self.slow) :]:
            results.append(fill(held[0][(0, 0)]))
        return jnp.concatenate([held[0][(0, 0)], held[1][(0, 0)]], axis=0), results

    def whole(self, block):
        found = {(0, 0): block}
        firsts = [self.step((0, 0), stage) for stage in self.slow]
        for name, stage in zip(firsts, self.slow):
            found[name] = self.swap(block, stage)
        return found

    def extend(self, found, turned):
        for stage in self.slow[::-1] if turned else self.slow:
            for name, value in list(found.items()):
                name = self.step(name, stage)
                if name not in found:
                    found[name] = self.swap(value, stage)

    def complete(self, found, turned, together=False):
        names = [name for name in found if name != (0, 0)]
        if together:
            found = {(0, 0): found[(0, 0)], **dict(zip(names, gate([found[name] for name in names])))}
        self.extend(found, turned)
        near = [found[name] for name in self.near]
        return [near + [self.swap(value) for value in near]]


def cut_of(count):
    return (count // 2 + 15) // 16 * 16


def columns_of(weight, groups, index, width, order=None):
    span = weight.shape[1] // groups
    order = range(groups) if order is None else order
    return jnp.concatenate(
        [lax.dynamic_slice_in_dim(weight, g * span + index * width, width, 1) for g in order], axis=1
    )


def allowed_of(plane, span_rows, own, lengths):
    places, slots = [], []
    for value in [v for _, v in plane.near + plane.far if _ == 0]:
        base = own ^ value
        rows = jnp.arange(span_rows, dtype=jnp.int32) + base * span_rows
        mem = jnp.arange(MEM_ROWS, dtype=jnp.int32) + base * MEM_ROWS
        places.append((rows, mem))
    far = jnp.int32(1 << 30)
    queries = jnp.concatenate([rows for rows, _ in places])
    keys = jnp.concatenate([jnp.concatenate([rows, jnp.where(mem < SUMM, -1, far)]) for rows, mem in places])
    causal = keys[None, :] <= queries[:, None]
    present = (keys[None, :] < lengths[:, None]) | (keys[None, :] >= SEG)
    return causal[None] & present[:, None, :]


def attend(query, key, value, allowed):
    scores = jnp.einsum("gqhd,gkhd->ghqk", query, key, preferred_element_type=f32)
    scores = jnp.where(allowed[:, None], scores, masked)
    largest = jnp.max(scores, axis=-1, keepdims=True)
    expanded = jnp.exp(scores - largest)
    totals = jnp.sum(expanded, axis=-1, keepdims=True)
    weights = (expanded / totals).astype(bf16)
    mixed = jnp.einsum("ghqk,gkhd->gqhd", weights, value, preferred_element_type=f32)
    return mixed.astype(bf16), largest + jnp.log(totals)


def attend_back(query, key, value, upstream, log_totals, allowed):
    scores = jnp.einsum("gqhd,gkhd->ghqk", query, key, preferred_element_type=f32)
    scores = jnp.where(allowed[:, None], scores, masked)
    weights = jnp.exp(scores - log_totals)
    value_grad = jnp.einsum("ghqk,gqhd->gkhd", weights.astype(bf16), upstream, preferred_element_type=f32)
    weight_grad = jnp.einsum("gqhd,gkhd->ghqk", upstream, value, preferred_element_type=f32)
    centre = jnp.sum(weights * weight_grad, axis=-1, keepdims=True)
    score_grad = (weights * (weight_grad - centre)).astype(bf16)
    query_grad = jnp.einsum("ghqk,gkhd->gqhd", score_grad, key, preferred_element_type=f32)
    key_grad = jnp.einsum("ghqk,gqhd->gkhd", score_grad, query, preferred_element_type=f32)
    return query_grad.astype(bf16) * 0.125, key_grad.astype(bf16), value_grad.astype(bf16)


def blocks_of(count):
    starts = list(range(0, count, QUERY_BLOCK))
    return [(s, min(QUERY_BLOCK, count - s)) for s in starts]


def piece_of(own, c):
    v = jnp.bitwise_xor(own, c)
    return jnp.right_shift(v, 1), jnp.bitwise_and(v, 1) == 0


def to_sequence(spans, span_rows, own, near, far, target, with_slots=True):
    base = spans * MEM_ROWS
    for c in range(spans):
        slot, is_near = piece_of(own, c)
        rows = jnp.where(is_near, near[slot, 0, :span_rows, :], far[slot, 0, :span_rows, :])
        target[base + c * span_rows : base + (c + 1) * span_rows] = rows
        if with_slots:
            rows = jnp.where(is_near, near[slot, 0, span_rows:, :], far[slot, 0, span_rows:, :])
            target[c * MEM_ROWS : (c + 1) * MEM_ROWS] = rows
    if not with_slots:
        target[:base] = jnp.zeros((base, target.shape[1]), target.dtype)


def key_bias(length, spans, seq_len):
    base = spans * MEM_ROWS
    shape = (base + seq_len, LANES)
    row = lax.broadcasted_iota(jnp.int32, shape, 0)
    place = row - base
    good = (row < SUMM) | ((place >= 0) & ((place < length) | (place >= SEG)))
    return jnp.where(good, 0.0, masked).astype(f32)


def head_masks(count):
    lane = lax.broadcasted_iota(jnp.int32, (count, LANES), 1)
    return lane < HEAD_DIM, lane == HEAD_DIM, lane == 0


def headed(array, masks, head):
    return jnp.where(masks[0] if head == 0 else ~masks[0], array, 0.0)


def scores_of(keys, query, start, size, base):
    stop = start + size
    scores = against(keys[:stop], query[start:stop])
    tail = scores[start:stop]
    row = lax.broadcasted_iota(jnp.int32, (size, size), 0)
    column = lax.broadcasted_iota(jnp.int32, (size, size), 1)
    seen = row <= column
    if start < base:
        seen = seen | (row < base - start)
    tail = jnp.where(seen, tail, masked)
    return tail if start == 0 else jnp.concatenate([scores[:start], tail], axis=0)


def attend_kernel(spans, span_rows, info, qn, qf, kn, kf, vn, vf, on, of, lse_ref, q_all, k_all, v_all, o_all):
    count = k_all.shape[0]
    base = spans * MEM_ROWS
    own = info[0]
    to_sequence(spans, span_rows, own, qn, qf, q_all)
    to_sequence(spans, span_rows, own, kn, kf, k_all)
    to_sequence(spans, span_rows, own, vn, vf, v_all)
    masks = head_masks(count)
    bias = key_bias(info[1 + pl.program_id(0)], spans, count - base)
    query, key = q_all[...].astype(f32), k_all[...].astype(f32)
    values = v_all[...].astype(f32).T.astype(bf16)
    queries, keys = [], []
    for head in range(2):
        flag = masks[1] if head == 0 else masks[2]
        queries.append((headed(query, masks, head) + jnp.where(flag, 1.0, 0.0)).astype(bf16))
        keys.append((headed(key, masks, head) + jnp.where(flag, bias, 0.0)).astype(bf16))
    for start, size in blocks_of(count):
        tops = []
        for head in range(2):
            scores = scores_of(keys[head], queries[head], start, size, base)
            largest = jnp.max(scores, axis=0, keepdims=True)
            expanded = jnp.exp(scores - largest)
            totals = jnp.sum(expanded, axis=0, keepdims=True)
            lse_ref[0, 0, head : head + 1, start : start + size] = largest + jnp.log(totals)
            mixed = jnp.dot(values[:, : start + size], expanded.astype(bf16), preferred_element_type=f32)
            tops.append(mixed[head * HEAD_DIM : (head + 1) * HEAD_DIM] / totals)
        o_all[start : start + size] = jnp.concatenate(tops, axis=0).T.astype(bf16)
    for c in range(spans):
        slot, is_near = piece_of(own, c)
        for target, chosen in ((on, is_near), (of, jnp.logical_not(is_near))):

            @pl.when(chosen)
            def _(c=c, slot=slot, target=target):
                target[slot, 0] = o_all[base + c * span_rows : base + (c + 1) * span_rows]


def attend_back_kernel(spans, span_rows, info, qn, qf, kn, kf, vn, vf, on, of, gn, gf, lse_ref, *rest):
    d_near, d_far, q_all, k_all, v_all, o_all, g_all, dq, dk, dv = rest[-10:]
    count = k_all.shape[0]
    base = spans * MEM_ROWS
    own = info[0]
    to_sequence(spans, span_rows, own, qn, qf, q_all)
    to_sequence(spans, span_rows, own, kn, kf, k_all)
    to_sequence(spans, span_rows, own, vn, vf, v_all)
    to_sequence(spans, span_rows, own, on, of, o_all, False)
    to_sequence(spans, span_rows, own, gn, gf, g_all, False)
    masks = head_masks(count)
    bias = key_bias(info[1 + pl.program_id(0)], spans, count - base)
    query, key, grad = q_all[...].astype(f32), k_all[...].astype(f32), g_all[...].astype(f32)
    overlap = (grad * o_all[...].astype(f32)).T
    keys_t = key.T.astype(bf16)
    values = v_all[...]
    plain_q, plain_g, flag_q, flag_k, deltas = [], [], [], [], []
    for head in range(2):
        flag = masks[1] if head == 0 else masks[2]
        own_q = headed(query, masks, head)
        plain_q.append(own_q.astype(bf16))
        plain_g.append(headed(grad, masks, head).astype(bf16))
        flag_q.append((own_q + jnp.where(flag, 1.0, 0.0)).astype(bf16))
        flag_k.append((headed(key, masks, head) + jnp.where(flag, bias, 0.0)).astype(bf16))
        deltas.append(jnp.sum(overlap[head * HEAD_DIM : (head + 1) * HEAD_DIM], axis=0, keepdims=True))
    for start, size in reversed(blocks_of(count)):
        stop = start + size
        tops, weights_low, slopes = [], [], []
        for head in range(2):
            scores = scores_of(flag_k[head], flag_q[head], start, size, base)
            weights = jnp.exp(scores - lse_ref[0, 0, head : head + 1, start:stop])
            weight_grad = against(values[:stop], plain_g[head][start:stop])
            slope = (weights * (weight_grad - deltas[head][:, start:stop])).astype(bf16)
            weights_low.append(weights.astype(bf16))
            slopes.append(slope)
            turned = jnp.dot(keys_t[:, :stop], slope, preferred_element_type=f32)
            tops.append(turned[head * HEAD_DIM : (head + 1) * HEAD_DIM])
        dq[start:stop] = (jnp.concatenate(tops, axis=0).T.astype(bf16).astype(f32) * 0.125).astype(bf16)
        grads = jnp.concatenate([plain_g[0][start:stop], plain_g[1][start:stop]], axis=0)
        queries = jnp.concatenate([plain_q[0][start:stop], plain_q[1][start:stop]], axis=0)
        value_part = jnp.dot(jnp.concatenate(weights_low, axis=1), grads, preferred_element_type=f32)
        key_part = jnp.dot(jnp.concatenate(slopes, axis=1), queries, preferred_element_type=f32)
        if stop == count:
            dv[...] = value_part
            dk[...] = key_part
        else:
            dv[:stop] += value_part
            dk[:stop] += key_part
    for c in range(spans):
        slot, is_near = piece_of(own, c)
        rows = slice(base + c * span_rows, base + (c + 1) * span_rows)
        slots = slice(c * MEM_ROWS, (c + 1) * MEM_ROWS)
        for target, chosen in ((d_near, is_near), (d_far, jnp.logical_not(is_near))):

            @pl.when(chosen)
            def _(slot=slot, rows=rows, slots=slots, target=target):
                for part, source in enumerate((dq, dk, dv)):
                    lanes = slice(part * LANES, (part + 1) * LANES)
                    target[slot, 0, :span_rows, lanes] = source[rows].astype(bf16)
                    low = jnp.zeros((MEM_ROWS, LANES), bf16) if part == 0 else source[slots].astype(bf16)
                    target[slot, 0, span_rows:, lanes] = low


def attend_call(info, near, far, span_rows, heads):
    slots, replicas, rows, _ = near.shape
    spans, pairs = 2 * slots, heads // 2
    count = spans * rows
    piece = lambda part: [pl.BlockSpec((slots, 1, rows, LANES), lambda r, p, info: (0, r, 0, 3 * p + part))] * 2
    mixed = pl.BlockSpec((slots, 1, span_rows, LANES), lambda r, p, info: (0, r, 0, p))
    shape = jax.ShapeDtypeStruct((slots, replicas, span_rows, pairs * LANES), bf16)
    return pl.pallas_call(
        functools.partial(attend_kernel, spans, span_rows),
        out_shape=(shape, shape, jax.ShapeDtypeStruct((replicas, pairs, 2, count), f32)),
        grid_spec=pltpu.PrefetchScalarGridSpec(
            num_scalar_prefetch=1,
            grid=(replicas, pairs),
            in_specs=piece(0) + piece(1) + piece(2),
            out_specs=(mixed, mixed, pl.BlockSpec((1, 1, 2, count), lambda r, p, info: (r, p, 0, 0))),
            scratch_shapes=[pltpu.VMEM((count, LANES), bf16)] * 4,
        ),
        compiler_params=pltpu.CompilerParams(vmem_limit_bytes=56 << 20),
        cost_estimate=pl.CostEstimate(flops=24 * 10**9, bytes_accessed=8 * 10**6, transcendentals=10**7),
        name="attend",
    )(info, near, far, near, far, near, far)


def attend_back_call(info, projected, attended, upstream, log_totals, span_rows, heads):
    slots, replicas, rows, _ = projected[0].shape
    spans, pairs = 2 * slots, heads // 2
    count = spans * rows
    piece = lambda part: [pl.BlockSpec((slots, 1, rows, LANES), lambda r, p, info: (0, r, 0, 3 * p + part))] * 2
    plain = [pl.BlockSpec((slots, 1, span_rows, LANES), lambda r, p, info: (0, r, 0, p))] * 4
    specs = piece(0) + piece(1) + piece(2) + plain
    specs.append(pl.BlockSpec((1, 1, 2, count), lambda r, p, info: (r, p, 0, 0)))
    inputs = [*projected, *projected, *projected, *attended, *upstream, log_totals]
    shape = jax.ShapeDtypeStruct((slots, replicas, rows, 3 * pairs * LANES), bf16)
    return pl.pallas_call(
        functools.partial(attend_back_kernel, spans, span_rows),
        out_shape=(shape, shape),
        grid_spec=pltpu.PrefetchScalarGridSpec(
            num_scalar_prefetch=1,
            grid=(replicas, pairs),
            in_specs=specs,
            out_specs=[pl.BlockSpec((slots, 1, rows, 3 * LANES), lambda r, p, info: (0, r, 0, p))] * 2,
            scratch_shapes=[pltpu.VMEM((count, LANES), bf16)] * 6 + [pltpu.VMEM((count, LANES), f32)] * 2,
        ),
        compiler_params=pltpu.CompilerParams(vmem_limit_bytes=56 << 20),
        cost_estimate=pl.CostEstimate(flops=30 * 10**9, bytes_accessed=16 * 10**6, transcendentals=10**7),
        name="attend_back",
    )(info, *inputs)


def place_up_kernel(owners, table, *refs):
    target = refs[-1]
    width = refs[0].shape[1] // owners
    team = target.shape[1] // (owners * width)
    for k in range(team):
        for z in range(owners):
            lanes = pl.ds(pl.multiple_of((z * team + table[k]) * width, width), width)
            target[:, lanes] = refs[k][:, z * width : (z + 1) * width].astype(f32)


def place_heads_kernel(order, table, *refs):
    target = refs[-1]
    groups = len(order)
    width = refs[0].shape[1] // groups
    team = target.shape[1] // (groups * width)
    half = team // 2
    odd = table[0] % 2 == 1
    for k in range(half):
        mine, other = refs[k][...].astype(f32), refs[k + half][...].astype(f32)
        first = jnp.where(odd, other, mine)
        second = jnp.where(odd, mine, other)
        place = table[k] // 2
        for position, g in enumerate(order):
            cut = slice(position * width, (position + 1) * width)
            lanes = pl.ds(pl.multiple_of((g * half + place) * 2 * width, 2 * width), 2 * width)
            target[:, lanes] = jnp.concatenate([first[:, cut], second[:, cut]], axis=1)


def place_columns(kernel, table, sides, rows, columns):
    result = None
    size = rows // len(sides)
    for number, side in enumerate(sides):
        inputs = list(side)
        if side[0].ndim == 3:
            block = (None, ROW_BLOCK, side[0].shape[2])
            specs = [pl.BlockSpec(block, lambda i, t, k=k: (k, i, 0)) for k in range(len(side))]
        else:
            specs = [pl.BlockSpec((ROW_BLOCK, side[0].shape[1]), lambda i, t: (i, 0))] * len(side)
        shift = number * size // ROW_BLOCK
        result = placed(kernel, table, inputs, specs, result, (rows, columns), (ROW_BLOCK, columns), size // ROW_BLOCK, lambda i, t: (i + shift, 0))
    return result


def placed(kernel, table, inputs, specs, result, shape, block, steps, index):
    aliases = {}
    if result is not None:
        inputs.append(result)
        specs.append(pl.BlockSpec(memory_space=pl.ANY))
        aliases = {len(inputs): 0}
    return pl.pallas_call(
        kernel,
        out_shape=jax.ShapeDtypeStruct(shape, f32),
        grid_spec=pltpu.PrefetchScalarGridSpec(
            num_scalar_prefetch=1,
            grid=(steps,),
            in_specs=specs,
            out_specs=pl.BlockSpec(block, index),
        ),
        input_output_aliases=aliases,
        compiler_params=pltpu.CompilerParams(vmem_limit_bytes=40 << 20),
        cost_estimate=pl.CostEstimate(flops=0, bytes_accessed=6 * steps * block[0] * block[1], transcendentals=0),
        name="place",
    )(table, *inputs)


def place_rows_kernel(team, table, *refs):
    target = refs[-1]
    for k in range(team):

        @pl.when(pl.program_id(0) == k)
        def _(k=k):
            target[...] = refs[k][...].astype(f32)


def place_rows(table, sides, used=None):
    team = len(sides[0])
    result = None
    count = len(sides)
    for number, side in enumerate(sides):
        size, columns = (used or side[0].shape[0]), side[0].shape[1]
        specs = [pl.BlockSpec((size, columns), lambda i, t: (0, 0), pipeline_mode=pl.Buffered(1))] * team
        kernel = functools.partial(place_rows_kernel, team)
        shape = (count * size * team, columns)
        result = placed(kernel, table, list(side), specs, result, shape, (size, columns), team, lambda i, t, number=number: (count * t[i] + number, 0))
    return result


def hold(value, *others):
    return lax.optimization_barrier((value, *others))[0]


def gate(values, *others):
    values = list(values)
    anywhere = pl.BlockSpec(memory_space=pl.ANY)
    return pl.pallas_call(
        lambda *refs: None,
        out_shape=[jax.ShapeDtypeStruct(v.shape, v.dtype) for v in values],
        in_specs=[anywhere] * (len(values) + len(others)),
        out_specs=[anywhere] * len(values),
        input_output_aliases={i: i for i in range(len(values))},
        name="gate",
    )(*values, *others)


def shards(
    hidden_in,
    memory_rows,
    seg_len,
    out_grad,
    first_gain,
    first_shift,
    qkv_weight,
    query_bias,
    value_bias,
    out_weight,
    out_bias,
    second_gain,
    second_shift,
    up_weight,
    up_bias,
    down_weight,
    down_bias,
):
    plane = Plane()
    owners = lax.axis_size("fsdp")
    replicas, spans = plane.replicas, plane.spans
    team = replicas * spans
    count = plane.half
    owner = lax.axis_index("fsdp")
    own_span = lax.axis_index("ctx")
    index = lax.axis_index("replica") * spans + own_span
    mate = jnp.bitwise_xor(index, 1)
    share = D // owners
    span_rows = hidden_in.shape[1]
    piece_rows = span_rows + MEM_ROWS
    heads = HEADS // team
    width = heads * HEAD_DIM
    hidden = up_bias.shape[0] // team
    ff = hidden * owners
    low = lambda array: array.astype(bf16)

    even = heads % owners == 0
    block = width // owners if even else width
    groups = owners if even else 1
    pairs = max(heads // 2, 1)
    inner = groups // pairs if groups > 1 else 1
    order = [part * groups + pair * inner + i for pair in range(pairs) for part in range(3) for i in range(inner)]
    columns_qkv = columns_of(qkv_weight, 3 * groups, index, block, order)
    weight_qkv = lax.all_gather(columns_qkv, "fsdp", axis=0, tiled=True)
    small = jnp.concatenate(
        [first_gain, first_shift, query_bias, value_bias, out_bias, second_gain, second_shift, down_bias, up_bias]
    )
    small = lax.all_gather(hold(small, columns_qkv).reshape(-1, 128), "fsdp", axis=0, tiled=True)
    small = small.reshape(owners, -1).astype(f32)
    vectors = [small[:, i * share : (i + 1) * share].reshape(D) for i in range(8)]
    gain_one, shift_one, bias_query, bias_value, bias_out, gain_two, shift_two, bias_down = vectors
    bias_up = jnp.concatenate(
        [lax.dynamic_slice_in_dim(small[:, 8 * share :], i * hidden, hidden, 1).reshape(ff) for i in (index, mate)]
    )
    if even:
        rows_out = lax.dynamic_slice_in_dim(out_weight, index * block, block, 0)
        weight_out = lax.all_gather(rows_out, "fsdp", axis=0, tiled=True)
    else:
        weight_out = lax.dynamic_slice_in_dim(
            lax.all_gather(out_weight, "fsdp", axis=0, tiled=True), index * width, width, 0
        )
    weight_up = lax.all_gather(columns_of(up_weight, owners, index, hidden), "fsdp", axis=0, tiled=True)
    weight_down = lax.all_gather(
        lax.dynamic_slice_in_dim(down_weight, index * hidden, hidden, 0), "fsdp", axis=0, tiled=True
    )
    with_mate = lambda weight, axis: jnp.concatenate([weight, plane.swap(weight)], axis=axis)

    cotangent = out_grad.reshape(span_rows, D)
    cot_float = cotangent.astype(f32)
    cot_first = plane.send(cotangent)

    tokens = hold(hidden_in, cot_first).reshape(span_rows, D)
    slots = jnp.pad(memory_rows.reshape(SUMM, D), ((0, spans * MEM_ROWS - SUMM), (0, 0)))
    slots = lax.dynamic_slice_in_dim(slots, own_span * MEM_ROWS, MEM_ROWS, 0)
    own_rows = jnp.concatenate([tokens, slots], axis=0).astype(f32)
    normal_one, inverse_one = normal_of(own_rows)
    lengths = [seg_len]
    for axis, bit in plane.slow:
        if axis == "replica":
            lengths = lengths + [plane.swap(v, (axis, bit)) for v in lengths]
    lengths = jnp.concatenate(lengths)

    normed, _ = plane.gather(hold(low(normal_one * gain_one + shift_one), lengths))
    weight_qkv = hold(weight_qkv, normed)
    qkv_mate = plane.swap(weight_qkv)
    bias_qkv = jnp.concatenate([bias_query, jnp.zeros((D,), f32), bias_value])[None]
    scale_qkv = jnp.asarray(np.repeat([0.125 if g < groups else 1.0 for g in order], block), f32)

    def project(rows, weight, device):
        bias = columns_of(bias_qkv, 3 * groups, device, block, order)[0]
        return low((dot(rows, weight) + bias) * scale_qkv).reshape(spans // 2, replicas, piece_rows, 3 * width)

    kernels = span_rows % 16 == 0 and heads % 2 == 0 and spans % 2 == 0 and SUMM <= spans * MEM_ROWS
    info = jnp.concatenate([own_span[None].astype(jnp.int32), lengths])
    split = lambda a: jnp.moveaxis(a, 1, 0).reshape(replicas, -1, heads, HEAD_DIM)
    to_pieces = lambda a: jnp.moveaxis(a.reshape(replicas, spans, -1, pairs, width // pairs), 0, 1)

    def parts_of(near, far):
        apart = jnp.concatenate([near, far], axis=0).reshape(spans, replicas, piece_rows, pairs, 3, width // pairs)
        return split(apart[:, :, :span_rows, :, 0]), split(apart[..., 1, :]), split(apart[..., 2, :])

    def attend_all():
        near, far = projected
        if kernels:
            return attend_call(info, near, far, span_rows, heads)
        allowed = allowed_of(plane, span_rows, own_span, lengths)
        mixed, totals = attend(*parts_of(near, far), allowed)
        mixed = to_pieces(mixed).reshape(spans, replicas, span_rows, width)
        return mixed[: spans // 2], mixed[spans // 2 :], totals

    projected = [project(normed, weight_qkv, index)]
    projected.append(plane.swap(project(normed, hold(qkv_mate, projected[0]), mate)))
    cot_all, filled = plane.gather(cotangent, (None, attend_all), cot_first)
    mixed_near, mixed_far, log_totals = filled[0]
    attended = jnp.concatenate([mixed_near, plane.swap(mixed_far)], axis=-1).reshape(count * span_rows, 2 * width)
    weight_out = with_mate(hold(weight_out, projected[0]), 0)
    branch, _ = plane.scatter(low(dot(attended, weight_out)))
    bias_out = gate([bias_out[None]], cot_all)[0][0] if kernels else bias_out
    weight_up = with_mate(gate([weight_up], branch)[0] if kernels else weight_up, 1)
    middle = tokens.astype(f32) + (branch + bias_out)
    normal_two, inverse_two = normal_of(middle)
    normed_two, _ = plane.gather(low(normal_two * gain_two + shift_two))

    upper = dot(normed_two, weight_up) + bias_up
    phi_up = 0.5 * (1.0 + lax.erf(upper * 0.7071067811865476))
    active = low(upper * phi_up)
    slope = low(phi_up + upper * (0.3989422804014327 * jnp.exp(-0.5 * upper * upper)))
    down_other = plane.swap(low(across(active[:, ff:], cot_all)))
    weight_down = with_mate(gate([weight_down], down_other)[0] if kernels else weight_down, 0)
    kept = []

    def upper_back(token):
        kept.append(low(against(cot_all, weight_down) * slope.astype(f32)))
        return kept[0]

    def normed_back(token):
        return low(against(kept[0], weight_up))

    feed = low(dot(active, weight_down))
    down_grad = low(across(active[:, :ff], cot_all) + down_other.astype(f32))
    down_mine = lax.psum_scatter(down_grad, "fsdp", scatter_dimension=0, tiled=True)
    feed, (upper_grad, partial) = plane.scatter(feed, (upper_back, normed_back))
    output = low(middle + (feed + bias_down))
    others = []

    later = [upper_grad]

    def mate_grads(token):
        if kernels:
            later[0] = gate([upper_grad], token)[0]
        others.append(plane.swap(low(across(normed_two, later[0][:, ff:]))))
        return others[0]

    normed_two_grad, _ = plane.scatter(partial, (None, mate_grads), (feed,) if kernels else ())
    up_other = gate([others[0]], down_mine)[0] if kernels else others[0]
    up_grad = low(across(normed_two, later[0][:, :ff]) + up_other.astype(f32))
    upper_grad = later[0]
    gain_back = gate([gain_two[None]], up_grad[:16])[0][0] if kernels else gain_two
    middle_grad = cot_float + norm_input_grad(normed_two_grad, normal_two, inverse_two, gain_back)
    branch_grad = low(middle_grad)
    up_mine = lax.psum_scatter(up_grad, "fsdp", scatter_dimension=0, tiled=True)
    up_bias_grad = jnp.sum(upper_grad.astype(f32), axis=0)
    branch_all, _ = plane.gather(branch_grad)

    shape = (spans // 2, replicas, span_rows, width)
    upstream_far = plane.swap(low(against(branch_all, weight_out[width:])))
    upstream_near = low(against(branch_all, weight_out[:width]))
    upstream = (upstream_near.reshape(shape), upstream_far.reshape(shape))
    fine = kernels and even and hidden % LANES == 0 and block * 2 == LANES and share % (2 * ROW_BLOCK) == 0
    if kernels:
        known = (info, projected, (mixed_near, mixed_far), upstream, log_totals, span_rows, heads)
        grads = attend_back_call(*known)
    else:
        allowed = allowed_of(plane, span_rows, own_span, lengths)
        upstream = split(jnp.concatenate(upstream, axis=0))
        query_grad, key_grad, value_grad = attend_back(*parts_of(*projected), upstream, log_totals, allowed)
        query_grad = jnp.pad(to_pieces(query_grad), ((0, 0), (0, 0), (0, MEM_ROWS), (0, 0), (0, 0)))
        grads = jnp.stack([query_grad, to_pieces(key_grad), to_pieces(value_grad)], axis=-2)
        grads = (grads[: spans // 2], grads[spans // 2 :])
    near, far = [g.reshape(count * piece_rows, 3 * width) for g in grads]
    if fine:
        down_found = plane.whole(gate([down_mine], upstream_near)[0])
        near, far = gate([near, far], *[v for name, v in down_found.items() if name != (0, 0)])
    other = plane.swap(far)
    qkv_grad = low(across(normed, near) + across(plane.swap(normed), far))
    if fine:
        qkv_grad = gate([qkv_grad], up_mine)[0]
    qkv_mine = lax.psum_scatter(qkv_grad, "fsdp", scatter_dimension=0, tiled=True)
    if fine:
        plane.extend(down_found, True)
        other = gate([other], qkv_grad, down_found[plane.near[-1]])[0]
    elif kernels:
        other = gate([other], qkv_grad)[0]
    both = jnp.concatenate([near, other], axis=1)
    partial = low(against(both, jnp.concatenate([weight_qkv, qkv_mate], axis=1)))
    def mate_out(token):
        others.append(low(across(attended[:, width:], hold(branch_all, token))))
        return others[-1]

    def own_out(token):
        return low(across(attended[:, :width], branch_all) + plane.swap(others[-1]).astype(f32))

    if fine:
        own_replica = lax.axis_index("replica")
        names = np.array(plane.near + plane.far, np.int32)
        table = jnp.bitwise_xor(own_replica, names[:, 0]) * spans + jnp.bitwise_xor(own_span, names[:, 1])
        table = table.astype(jnp.int32)
    normed_grad, (_, out_grad_w) = plane.scatter(partial, (mate_out, own_out))
    rows_grad = norm_input_grad(normed_grad, normal_one, inverse_one, gain_one)
    input_grad = middle_grad + rows_grad[:span_rows]
    slots_all = {0: rows_grad[span_rows:]}
    bit = 1
    while bit < spans:
        for value, rows in list(slots_all.items()):
            slots_all[value ^ bit] = plane.swap(rows, ("ctx", bit))
        bit *= 2
    slots_grad = jnp.zeros((spans * MEM_ROWS, D), f32)
    for value, rows in slots_all.items():
        start = jnp.bitwise_xor(own_span, value) * MEM_ROWS
        slots_grad = lax.dynamic_update_slice_in_dim(slots_grad, rows, start, 0)
    slots_grad = slots_grad[:SUMM]

    def spot(values, full, groups, size, device):
        base = jnp.zeros((groups, full // groups), f32)
        return lax.dynamic_update_slice_in_dim(base, values.reshape(groups, size), device * size, 1).reshape(full)

    bias_grads = (jnp.sum(near.astype(f32), axis=0) + jnp.sum(far.astype(f32), axis=0)).reshape(pairs, 3, -1)
    parts = [
        spot(bias_grads[:, 0], D, groups, block, index),
        spot(bias_grads[:, 2], D, groups, block, index),
        jnp.sum(branch_grad.astype(f32), axis=0),
        jnp.sum(normed_two_grad * normal_two, axis=0),
        jnp.sum(normed_two_grad, axis=0),
        jnp.sum(cot_float, axis=0),
        spot(up_bias_grad[:ff], ff * team, owners, hidden, index)
        + spot(up_bias_grad[ff:], ff * team, owners, hidden, mate),
    ]
    sums = jnp.sum(partial.astype(f32), axis=0)
    parts += [(jnp.sum(partial.astype(f32) * normed.astype(f32), axis=0) - shift_one * sums) / gain_one, sums]
    vector = low(jnp.concatenate([part.reshape(owners, -1) for part in parts], axis=1))
    used = vector.shape[1]
    extra = -(-used // (16 * D)) * 16
    vector = jnp.pad(vector, ((0, 0), (0, extra * D - used))).reshape(owners, extra, D)

    def columns_all(full, groups, size):
        full = full.reshape(team, share, groups, size)
        return jnp.moveaxis(full, 0, 2).reshape(share, -1).astype(f32)

    if fine:
        qkv_found = plane.whole(qkv_mine)
        down_all = place_rows(table, plane.complete(down_found, True))
        sides = plane.complete(qkv_found, True, True)
        devices = jnp.arange(team, dtype=jnp.int32)
        up_full = lax.all_gather(gate([up_mine], qkv_mine)[0], PLANE, axis=0, tiled=False)
        up_all = place_columns(
            functools.partial(place_up_kernel, owners), devices, [[up_full] * team], share, ff * team
        )
        out_rows = gate([out_grad_w], qkv_mine)[0].reshape(owners, block, D)
        joined = jnp.concatenate([out_rows, vector], axis=1).reshape(-1, D)
        out_mine = lax.psum_scatter(joined, "fsdp", scatter_dimension=0, tiled=True)
        qkv_all = place_columns(functools.partial(place_heads_kernel, order), table, sides, share, 3 * D)
        out_mine = gate([out_mine], down_all, *[v for name, v in qkv_found.items() if name != (0, 0)])[0]
        out_sides = plane.complete(plane.whole(out_mine), False)
        out_all = place_rows(table, out_sides, block)
        vectors = sum(rows[block:].astype(f32) for rows in out_sides[0])
    else:
        down_all = lax.all_gather(down_mine, PLANE, axis=0, tiled=True).astype(f32)
        up_all = columns_all(lax.all_gather(up_mine, PLANE, axis=0, tiled=False), owners, hidden)
        qkv_full = lax.all_gather(qkv_mine, PLANE, axis=0, tiled=False).reshape(team, share, 3 * groups, block)
        qkv_full = jnp.concatenate([qkv_full[:, :, order.index(g)][:, :, None] for g in range(3 * groups)], axis=2)
        qkv_all = columns_all(qkv_full, 3 * groups, block)
        if even:
            out_mine = lax.psum_scatter(out_grad_w, "fsdp", scatter_dimension=0, tiled=True)
            out_all = lax.all_gather(out_mine, PLANE, axis=0, tiled=True).astype(f32)
        else:
            placed = lax.dynamic_update_slice_in_dim(jnp.zeros((D, D), bf16), out_grad_w, index * width, 0)
            out_all = lax.psum(lax.psum_scatter(placed, "fsdp", scatter_dimension=0, tiled=True), PLANE).astype(f32)
        vectors = lax.psum(lax.psum_scatter(vector, "fsdp", scatter_dimension=0, tiled=True), PLANE).astype(f32)
    vectors = vectors.reshape(-1)
    take = lambda i: vectors[i * share : (i + 1) * share]
    up_end = 6 * share + ff * team // owners
    return (
        output.reshape(hidden_in.shape),
        input_grad.reshape(hidden_in.shape),
        slots_grad.reshape(memory_rows.shape),
        vectors[up_end : up_end + share],
        vectors[up_end + share : up_end + 2 * share],
        qkv_all,
        take(0),
        take(1),
        out_all,
        take(2),
        take(3),
        take(4),
        up_all,
        vectors[6 * share : up_end],
        down_all,
        take(5),
    )


def solution(mesh):
    rows = P(("fsdp", "replica"), "ctx", None)
    part = P("fsdp")
    table = P("fsdp", None)
    whole = P(("fsdp", "replica"), None, None)
    return jax.shard_map(
        shards,
        mesh=mesh,
        in_specs=(
            rows,
            whole,
            P(("fsdp", "replica")),
            rows,
            part,
            part,
            table,
            part,
            part,
            table,
            part,
            part,
            part,
            table,
            part,
            table,
            part,
        ),
        out_specs=(
            rows,
            rows,
            whole,
            part,
            part,
            table,
            part,
            part,
            table,
            part,
            part,
            part,
            table,
            part,
            table,
            part,
        ),
        check_vma=False,
    )
```
